256 devices in a mesh: img: 16 (over z, core), depth: 16 (over y, x).
Axes of the slice: x: 4, y: 4, z: 8, core: 2. Of those that a mesh axis runs over, the one named last changes fastest.
Arguments:
- volume: bfloat16 [64, 1024, 1024], P('depth', 'img'), may hold values from 0 to 1
- entry_depth: int32 [1024, 1024], P('img'), may hold values from 0 to 63
- tf_table: float32 [256, 4], replicated, may hold values from 0.1 to 4
Outputs:
- image: float32 [4, 1024, 1024], P(None, 'depth', 'img')
The draws below stay inside these ranges and needn't reach their ends.
All inputs are finite; a program needn't handle non-finite values.
Results may differ from the reference program's by a relative error of at most 0.0003.
Values may be sent and summed in bfloat16 or wider, within the bound.
A program may use at most 64 MiB of HBM per device.

```python
import math
import jax
import jax.numpy as jnp
from jax import lax

NY = 1024
K = 256
NX = 1024
NZ = 64
N_IMG = 16


def set_ends(array, own_key, least, largest):
    extent = array.shape
    index_at = [jax.random.randint(jax.random.fold_in(own_key, axis), (), 0, extent[axis]) for axis in range(len(extent))]
    array = array.at[tuple(index_at)].set(least)
    longest = extent.index(max(extent))
    index_at[longest] = (index_at[longest] + 1) % extent[longest]
    return array.at[tuple(index_at)].set(largest)


def levels(rng, dims, pieces, low, high):
    def one(position, blocks):
        steps = jax.random.uniform(jax.random.fold_in(jax.random.fold_in(rng, 6), position), (blocks,), jnp.float32, low / len(pieces), high / len(pieces))
        return jnp.repeat(jnp.exp(steps), dims[position] // blocks).reshape((-1,) + (1,) * (len(dims) - position - 1))

    factor_of = one(*pieces[0])
    for cut in pieces[1:]:
        factor_of = factor_of * one(*cut)
    return factor_of


def setup_inputs(seed: int = 0) -> dict:
    arg_keys = jax.random.split(jax.random.key(seed), 4)
    return {
        "volume": jnp.clip(1.0 * jax.random.uniform(arg_keys[0], (NZ, NX, NY), jnp.float32) ** levels(arg_keys[0], (NZ, NX, NY), ((0, 16), (1, 16)), -0.2, 0.2), 0.0, 1.0).astype(jnp.bfloat16),
        "entry_depth": set_ends(jax.random.randint(arg_keys[1], (NX, NY), 0, NZ), jax.random.fold_in(arg_keys[1], 1), 0, NZ - 1).astype(jnp.int32),
        "tf_table": jnp.clip(jnp.exp(jax.random.uniform(arg_keys[2], (K, 4), jnp.float32, math.log(0.1), math.log(4.0))), 0.1, 4.0),
    }


def transfer(sample, tf_table):
    bins = tf_table.shape[0]
    scaled = sample * (bins - 1)
    lower = jnp.clip(jnp.floor(scaled).astype(jnp.int32), 0, bins - 2)
    frac = scaled - lower.astype(scaled.dtype)
    table_rows = tf_table.T
    channels = []
    for channel_id in range(4):
        low_value = jnp.take(table_rows[channel_id], lower)
        high_value = jnp.take(table_rows[channel_id], lower + 1)
        channels.append(low_value + frac * (high_value - low_value))
    return channels


def reference(volume, entry_depth, tf_table):
    padded = jnp.pad(volume, ((0, 1), (0, 1), (0, 1)))
    block_width = NX // N_IMG
    depth_pos = jnp.arange(NZ, dtype=jnp.int32)[:, None, None]

    def one_block(block_index):
        first_col = (block_index * block_width).astype(jnp.int32)
        column_block = lax.dynamic_slice_in_dim(padded, first_col, block_width + 1, 1).astype(jnp.float32)
        depth_sum = column_block[:-1] + column_block[1:]
        column_sum = depth_sum[:, :-1] + depth_sum[:, 1:]
        sample = (column_sum[:, :, :-1] + column_sum[:, :, 1:]) * 0.125
        entry_block = lax.dynamic_slice_in_dim(entry_depth, first_col, block_width, 0)
        colour = transfer(sample, tf_table)
        optical = jnp.where(depth_pos >= entry_block[None], colour[3] * (2.0 / NZ), 0.0)
        opacity = 1.0 - jnp.exp(-optical)
        before = jnp.cumsum(optical, axis=0) - optical
        weight = jnp.exp(-before) * opacity
        planes = [jnp.sum(weight * colour[channel_id], axis=0) for channel_id in range(3)]
        planes.append(jnp.exp(-jnp.sum(optical, axis=0)))
        return jnp.stack(planes)

    blocks = lax.map(one_block, jnp.arange(N_IMG, dtype=jnp.int32))
    return jnp.transpose(blocks, (1, 3, 0, 2)).reshape(4, NY, NX)
```

```python
import math

import jax
import jax.numpy as jnp
from jax import lax
from jax.experimental import pallas as pl
from jax.experimental.pallas import tpu as pltpu
from jax.sharding import PartitionSpec as P

MESH = pl.DeviceIdType.MESH
F32, BF16, I32 = jnp.float32, jnp.bfloat16, jnp.int32
ND = 16
NI = 16
ZB = 4
XB = 64
XH = 32
YB = 64
LANES = 128
HALO = 8
BODY = ZB * XH
ROWS = HALO + BODY
KROWS = ROWS + HALO + XH
ORDER = sorted(range(1, ND), key=lambda k: -((0, 1, 2, 1)[k & 3] + (0, 1, 2, 1)[k >> 2]))


def iota(shape, axis):
    return lax.broadcasted_iota(I32, shape, axis)


def zero_one(mask):
    return jnp.where(mask, 1.0, 0.0).astype(BF16)


def nt_dot(a, b, precision=None):
    return lax.dot_general(
        a, b, (((1,), (1,)), ((), ())), preferred_element_type=F32, precision=precision
    )


def halves(a, b, low):
    turned = pltpu.roll(jnp.where(low, b, a), YB, 1)
    return jnp.where(low, a, turned), jnp.where(low, turned, b)


def band_matrix():
    row = iota((BODY, KROWS), 0)
    col = iota((BODY, KROWS), 1)
    z, x = row // XH, row % XH
    nxt = col >= ROWS
    local = jnp.where(nxt, col - ROWS, col)
    is_halo = local < HALO
    zz = jnp.where(nxt, ZB, 0) + jnp.where(is_halo, local, (local - HALO) // XH)
    used = jnp.logical_or(jnp.logical_not(is_halo), local < jnp.where(nxt, 1, ZB))
    xx = jnp.where(is_halo, XH, (local - HALO) % XH)
    dz, dx = zz - z, xx - x
    near = (dz >= 0) & (dz <= 1) & (dx >= 0) & (dx <= 1)
    return zero_one(near & used)


def kernel(
    vol, entry, table, out,
    vbuf, ebuf, cbuf, pk, rb, tabs, edge, ent, band,
    vsem, esem, lsem, csend, crecv, msend, mrecv, hsend, hrecv,
):
    me = lax.axis_index("depth")
    im = lax.axis_index("img")
    left = lax.rem(im + NI - 1, NI)
    right = lax.rem(im + 1, NI)

    barrier = pltpu.get_barrier_semaphore()
    for k in ORDER:
        pl.semaphore_signal(barrier, 1, device_id={"img": im, "depth": me ^ k}, device_id_type=MESH)
    for side in (left, right):
        pl.semaphore_signal(barrier, 1, device_id={"img": side, "depth": me}, device_id_type=MESH)

    load_vol = pltpu.make_async_copy(vol, vbuf, vsem)
    load_vol.start()
    group = pl.multiple_of((me // 2) * LANES, LANES)
    load_entry = pltpu.make_async_copy(entry.at[:, pl.ds(group, LANES)], ebuf, esem)
    load_entry.start()

    low = iota((XH, LANES), 1) < YB
    low8 = iota((8, LANES), 1) < YB

    load_vol.wait()
    for g in range(ND // 2):
        lanes = slice(LANES * g, LANES * (g + 1))
        for z in range(ZB):
            a, b = halves(vbuf[z, 0:XH, lanes], vbuf[z, XH:XB, lanes], low)
            pk[2 * g, HALO + XH * z : HALO + XH * (z + 1), :] = a
            pk[2 * g + 1, HALO + XH * z : HALO + XH * (z + 1), :] = b

    pl.semaphore_wait(barrier, ND - 1 + 2)

    send_col = pltpu.make_async_remote_copy(
        vbuf.at[:, pl.ds(0, 8), :], cbuf, csend, crecv,
        device_id={"img": left, "depth": me}, device_id_type=MESH,
    )
    send_col.start()

    def main_copy(k):
        return pltpu.make_async_remote_copy(
            pk.at[me ^ k, pl.ds(HALO, BODY), :],
            rb.at[me, pl.ds(HALO, BODY), :],
            msend.at[k], mrecv.at[k],
            device_id={"img": im, "depth": me ^ k}, device_id_type=MESH,
        )

    def halo_copy(k):
        return pltpu.make_async_remote_copy(
            pk.at[me ^ k, pl.ds(0, HALO), :],
            rb.at[me, pl.ds(0, HALO), :],
            hsend.at[k], hrecv.at[k],
            device_id={"img": im, "depth": me ^ k}, device_id_type=MESH,
        )

    for k in ORDER:
        main_copy(k).start()

    sel_row = iota((LANES, ND * YB), 0)
    sel_col = iota((LANES, ND * YB), 1)
    hit = sel_col == (sel_row // 8) * YB + YB
    kind = sel_row % 8
    columns = vbuf[...].reshape(ZB * XB, ND * YB)
    rows45 = nt_dot(zero_one(hit & (kind == 4)), columns[:LANES])
    rows45 += nt_dot(zero_one(hit & (kind == 5)), columns[LANES:])
    send_col.wait_recv()
    last = im == NI - 1
    col = [jnp.where(last, 0.0, cbuf[z, 0:1, :].astype(F32)) for z in range(ZB)]
    zero_row = jnp.zeros((1, ND * YB), F32)
    xb = jnp.concatenate(col + [zero_row] * 4, 0)
    xa = jnp.concatenate([vbuf[z, XH : XH + 1, :].astype(F32) for z in range(ZB)] + [zero_row] * 4, 0)
    zcol = iota((LANES, ND * YB), 0)

    def corner_rows(first):
        a = jnp.broadcast_to(col[first], (LANES, ND * YB))
        b = jnp.broadcast_to(col[first + 1], (LANES, ND * YB))
        return jnp.where(zcol == 0, a, jnp.where(zcol == YB, b, 0.0)).astype(BF16)

    rows45 += nt_dot(zero_one(hit & (kind == 6)), corner_rows(0))
    rows45 += nt_dot(zero_one(hit & (kind == 7)), corner_rows(2))
    for g in range(ND // 2):
        lanes = slice(LANES * g, LANES * (g + 1))
        a, b = halves(xa[:, lanes], xb[:, lanes], low8)
        pk[2 * g, 0:HALO, :] = (a + rows45[16 * g : 16 * g + 8]).astype(BF16)
        pk[2 * g + 1, 0:HALO, :] = (b + rows45[16 * g + 8 : 16 * g + 16]).astype(BF16)
    for k in ORDER:
        halo_copy(k).start()
    own = pltpu.make_async_copy(pk.at[me], rb.at[me], lsem)
    own.start()

    rb[ND] = jnp.zeros((ROWS, LANES), BF16)

    eye = jnp.where(iota((8, 4), 0) == iota((8, 4), 1), 1.0, 0.0)
    by_channel = nt_dot(eye, table[...], lax.Precision.HIGHEST)
    lo_half, hi_half = by_channel[:, :LANES], by_channel[:, LANES:]
    last_lane = iota((8, LANES), 1) == LANES - 1
    lo_next = jnp.where(last_lane, pltpu.roll(hi_half, LANES - 1, 1), pltpu.roll(lo_half, LANES - 1, 1))
    lo_next = jnp.where(last_lane, jnp.broadcast_to(hi_half[:, 0:1], (8, LANES)), lo_next)
    hi_next = jnp.where(last_lane, hi_half, pltpu.roll(hi_half, LANES - 1, 1))
    scale = -2.0 / (ND * ZB) * math.log2(math.e)
    for c in range(4):
        for part, rows in enumerate((lo_half, hi_half, lo_next - lo_half, hi_next - hi_half)):
            row = jnp.broadcast_to(rows[c : c + 1], (8, LANES))
            tabs[4 * c + part] = row * scale if c == 3 else row

    band[...] = band_matrix()

    load_entry.wait()
    e0, e1 = ebuf[0:XH, :], ebuf[XH:XB, :]
    even, odd = halves(e0, e1, low)
    ent[...] = jnp.where(lax.rem(me, 2) == 0, even, odd)

    own.wait()
    for k in ORDER:
        main_copy(k).wait_recv()
    for k in ORDER:
        halo_copy(k).wait_recv()

    tiles = jnp.concatenate([rb[d, 0:HALO, :] for d in range(ND)], 0)
    r = iota((LANES, LANES), 0)
    lane = iota((LANES, LANES), 1)
    q, hx = r // 64, r % 64
    dx = lane % 64 - hx
    sums = nt_dot(zero_one((lane // 64 == q) & (dx >= 0) & (dx <= 1)), tiles)
    corner = nt_dot(zero_one((lane == q * 64) & (hx == 63)), tiles)
    sums += pltpu.roll(corner, LANES - 2, 1)
    p0, p1 = sums[:64], sums[64:]
    lane64 = iota((64, LANES), 1)
    nxt = jnp.where(
        lane64 % 8 == 4,
        pltpu.roll(p0, LANES - 1, 1),
        jnp.where(lane64 >= LANES - 7, 0.0, pltpu.roll(p0, LANES - 7, 1)),
    )
    for par, e in enumerate((p0 + p1, p1 + nxt)):
        ea, eb = e[:XH], e[XH:]
        first, second = halves(ea, eb, low)
        edge[par, 0] = first
        edge[par, 1] = second

    is_edge = (iota((8, LANES), 1) & (YB - 1)) == YB - 1
    tiles_x = XH // 8
    zero = jnp.zeros((8, LANES), F32)
    one = jnp.ones((8, LANES), F32)

    def lookup(sample, tab):
        scaled = sample * 31.875
        lower = jnp.minimum(jnp.floor(scaled), 254.0)
        frac = scaled - lower
        index = lower.astype(I32)
        high = index >= LANES
        within = index & (LANES - 1)
        values = []
        for c in range(4):
            t = [jnp.take_along_axis(tab[4 * c + p], within, axis=1, mode="promise_in_bounds") for p in range(4)]
            values.append(jnp.where(high, t[1], t[0]) + frac * jnp.where(high, t[3], t[2]))
        return values

    def brick(d, carry):
        cum, bright, acc = carry
        cum, bright = list(cum), list(bright)
        acc = [list(a) for a in acc]
        data = jnp.concatenate([rb[d], rb[d + 1, 0 : HALO + XH, :]], 0)
        s = jnp.dot(band[...], data, preferred_element_type=F32)
        tab = [tabs[i] for i in range(16)]
        side = d // 8
        base = (d - side * 8) * 8
        for z in range(ZB):
            shift = lax.rem(YB - 1 - (base + 4 + z // 2) + LANES, LANES)
            for t in range(tiles_x):
                here = s[XH * z + 8 * t : XH * z + 8 * t + 8]
                beyond = pltpu.roll(edge[z % 2, side, 8 * t : 8 * t + 8, :], shift, 1)
                below = jnp.where(is_edge, beyond, pltpu.roll(here, LANES - 1, 1))
                colour = lookup(here + below, tab)
                inside = ent[8 * t : 8 * t + 8, :] <= ZB * d + z
                cum[t] = cum[t] + jnp.where(inside, colour[3], 0.0)
                bright_next = jnp.exp2(cum[t])
                weight = bright[t] - bright_next
                bright[t] = bright_next
                for c in range(3):
                    acc[c][t] = acc[c][t] + weight * colour[c]
        return tuple(cum), tuple(bright), tuple(tuple(a) for a in acc)

    start = ((zero,) * tiles_x, (one,) * tiles_x, ((zero,) * tiles_x,) * 3)
    _, bright, acc = lax.fori_loop(0, ND, brick, start)
    planes = jnp.concatenate([v for a in acc for v in a] + list(bright), 0)
    turned = planes.T
    for c in range(4):
        for h in range(2):
            out[c, :, XH * h : XH * (h + 1)] = turned[YB * h : YB * (h + 1), XH * c : XH * (c + 1)]

    for k in ORDER:
        main_copy(k).wait_send()
        halo_copy(k).wait_send()
    send_col.wait_send()


def shards(volume, entry_depth, tf_table):
    dma = pltpu.SemaphoreType.DMA
    return pl.pallas_call(
        kernel,
        out_shape=jax.ShapeDtypeStruct((4, YB, XB), F32),
        in_specs=[
            pl.BlockSpec(memory_space=pl.ANY),
            pl.BlockSpec(memory_space=pl.ANY),
            pl.BlockSpec(memory_space=pltpu.VMEM),
        ],
        out_specs=pl.BlockSpec(memory_space=pltpu.VMEM),
        scratch_shapes=[
            pltpu.VMEM((ZB, XB, ND * YB), BF16),
            pltpu.VMEM((XB, LANES), I32),
            pltpu.VMEM((ZB, 8, ND * YB), BF16),
            pltpu.VMEM((ND, ROWS, LANES), BF16),
            pltpu.VMEM((ND + 1, ROWS, LANES), BF16),
            pltpu.VMEM((16, 8, LANES), F32),
            pltpu.VMEM((2, 2, XH, LANES), F32),
            pltpu.VMEM((XH, LANES), I32),
            pltpu.VMEM((BODY, KROWS), BF16),
            dma, dma, dma, dma, dma,
            dma((ND,)), dma((ND,)), dma((ND,)), dma((ND,)),
        ],
        compiler_params=pltpu.CompilerParams(collective_id=0, has_side_effects=True),
        name="render",
    )(volume, entry_depth, tf_table)


def solution(mesh):
    placed = (P("depth", "img", None), P("img", None), P())
    return jax.shard_map(
        shards, mesh=mesh, in_specs=placed, out_specs=P(None, "depth", "img"), check_vma=False
    )
```

```python
import math

import jax
import jax.numpy as jnp
from jax import lax
from jax.experimental import pallas as pl
from jax.experimental.pallas import tpu as pltpu
from jax.sharding import PartitionSpec as P

MESH = pl.DeviceIdType.MESH
F32, BF16, I32 = jnp.float32, jnp.bfloat16, jnp.int32
ND = 16
NI = 16
ZB = 4
XB = 64
XH = 32
YB = 64
NY = ND * YB
LANES = 128
TILE = 8
BODY = ZB * XH
ROWS = BODY + TILE
KROWS = BODY + XH + 2 * TILE
XT = XH // 8
SCALE = 255.0 / 8.0
UNIT = 2.0 / 65535.0
OPTICAL = -2.0 / (ND * ZB) * math.log2(math.e) * UNIT * UNIT
ORDER = sorted(range(1, ND), key=lambda k: -((0, 1, 2, 1)[k & 3] + (0, 1, 2, 1)[k >> 2]))


def iota(shape, axis):
    return lax.broadcasted_iota(I32, shape, axis)


def choose(mask, value=1.0):
    return jnp.where(mask, value, 0.0).astype(BF16)


def nt_dot(a, b):
    return lax.dot_general(a, b, (((1,), (1,)), ((), ())), preferred_element_type=F32)


def nn_dot(a, b):
    return jnp.dot(a, b, preferred_element_type=F32)


def halves(a, b, low):
    turned = pltpu.roll(jnp.where(low, b, a), YB, 1)
    return jnp.where(low, a, turned), jnp.where(low, turned, b)


def band_matrix():
    row = iota((BODY, KROWS), 0)
    col = iota((BODY, KROWS), 1)
    z, x = row // XH, row % XH
    tile = col - (BODY + XH)
    in_tile = tile >= 0
    part = tile % TILE - ZB
    zz = jnp.where(in_tile, jnp.where(tile >= TILE, ZB + part, part), col // XH)
    used = (tile < 0) | ((tile < TILE) & (part >= 0)) | ((tile >= TILE) & (part == 0))
    xx = jnp.where(in_tile, XH, col % XH)
    dz, dx = zz - z, xx - x
    near = (dz >= 0) & (dz <= 1) & (dx >= 0) & (dx <= 1)
    return choose(near & used, SCALE)


def kernel(
    vol, entry, table, out,
    vbuf, ebuf, pk, ck, rb, cb, words, ent, band, pair,
    vsem, esem, msend, hsend, csend, mrecv, crecv,
):
    me = lax.axis_index("depth")
    im = lax.axis_index("img")
    left = jnp.maximum(im - 1, 0)
    right = jnp.minimum(im + 1, NI - 1)
    has_left, has_right = im > 0, im < NI - 1

    load_vol = pltpu.make_async_copy(vol, vbuf, vsem)
    load_vol.start()
    group = pl.multiple_of((me // 2) * LANES, LANES)
    load_entry = pltpu.make_async_copy(entry.at[:, pl.ds(group, LANES)], ebuf, esem)
    load_entry.start()

    barrier = pltpu.get_barrier_semaphore()
    for k in ORDER:
        pl.semaphore_signal(barrier, 1, device_id={"img": im, "depth": me ^ k}, device_id_type=MESH)

    @pl.when(has_right)
    def _():
        for k in range(ND):
            pl.semaphore_signal(barrier, 1, device_id={"img": right, "depth": me ^ k}, device_id_type=MESH)

    low = iota((XH, LANES), 1) < YB
    low8 = iota((TILE, LANES), 1) < YB

    load_vol.wait()
    for g in range(ND // 2):
        lanes = slice(LANES * g, LANES * (g + 1))
        for z in range(ZB):
            a, b = halves(vbuf[z, 0:XH, lanes], vbuf[z, XH:XB, lanes], low)
            pk[2 * g, XH * z : XH * (z + 1), :] = a
            pk[2 * g + 1, XH * z : XH * (z + 1), :] = b

    pl.semaphore_wait(barrier, jnp.where(has_left, 2 * ND - 1, ND - 1))

    for k in ORDER:
        pltpu.make_async_remote_copy(
            pk.at[me ^ k, pl.ds(0, BODY), :], rb.at[me, pl.ds(0, BODY), :], msend, mrecv.at[me],
            device_id={"img": im, "depth": me ^ k}, device_id_type=MESH,
        ).start()

    sel = choose(iota((ND, NY), 1) == iota((ND, NY), 0) * YB + YB)
    zero_row = jnp.zeros((1, NY), F32)
    first = jnp.concatenate([vbuf[z, 0:1, :].astype(F32) for z in range(ZB)] + [zero_row] * 4, 0)
    middle = jnp.concatenate([zero_row] * 4 + [vbuf[z, XH : XH + 1, :].astype(F32) for z in range(ZB)], 0)
    by_row = nt_dot(sel, vbuf[...].reshape(ZB * XB, NY)).astype(BF16)
    corner = nt_dot(sel, first.astype(BF16))
    spot = iota((LANES, ND), 0)
    block = iota((LANES, ND), 1)
    lane = iota((LANES, LANES), 1)
    mine = jnp.zeros((LANES, LANES), F32)
    corner = corner.astype(BF16)
    spread = nn_dot(choose(spot // TILE == block), corner)
    at_corner = jnp.zeros((LANES, LANES), F32)
    tile_row = iota((LANES, LANES), 0) % TILE
    for z in range(ZB):
        place = choose((spot // TILE == block) & (spot % TILE == z))
        half = by_row[:, LANES * (z // 2) : LANES * (z // 2 + 1)]
        part = nn_dot(place, half)
        if z % 2:
            part = pltpu.roll(part, YB, 1)
        mine += jnp.where(lane < YB, part, 0.0)
        at_corner += jnp.where((lane == YB) & (tile_row == z), jnp.broadcast_to(spread[:, z : z + 1], (LANES, LANES)), 0.0)
    first = pltpu.roll(first, 4, 0)
    for g in range(ND // 2):
        lanes = slice(LANES * g, LANES * (g + 1))
        a = middle[:, lanes]
        b = first[:, lanes]
        even, odd = slice(2 * TILE * g, 2 * TILE * g + TILE), slice(2 * TILE * g + TILE, 2 * TILE * (g + 1))
        turned = pltpu.roll(jnp.where(low8, b, a), YB, 1)
        pk[2 * g, BODY:ROWS, :] = (mine[even] + jnp.where(low8, a, 0.0)).astype(BF16)
        pk[2 * g + 1, BODY:ROWS, :] = (mine[odd] + jnp.where(low8, turned, 0.0)).astype(BF16)
        ck[2 * g] = (at_corner[even] + jnp.where(low8, 0.0, turned)).astype(BF16)
        ck[2 * g + 1] = (at_corner[odd] + jnp.where(low8, 0.0, b)).astype(BF16)

    for k in ORDER:
        pltpu.make_async_remote_copy(
            pk.at[me ^ k, pl.ds(BODY, TILE), :], rb.at[me, pl.ds(BODY, TILE), :], hsend, mrecv.at[me],
            device_id={"img": im, "depth": me ^ k}, device_id_type=MESH,
        ).start()

    @pl.when(has_left)
    def _():
        for k in range(ND):
            pltpu.make_async_remote_copy(
                ck.at[me ^ k], cb.at[me], csend, crecv.at[me],
                device_id={"img": left, "depth": me ^ k}, device_id_type=MESH,
            ).start()

    pltpu.make_async_copy(pk.at[me], rb.at[me], mrecv.at[me]).start()

    rb[ND] = jnp.zeros((ROWS, LANES), BF16)
    cb[ND] = jnp.zeros((TILE, LANES), BF16)

    @pl.when(jnp.logical_not(has_right))
    def _():
        cb[0:ND] = jnp.zeros((ND, TILE, LANES), BF16)

    code = jnp.floor(jnp.sqrt(table[...]) * (1.0 / UNIT) + 0.5)
    code_lo, code_hi = code[:, :LANES], code[:, LANES:]
    last_lane = iota((4, LANES), 1) == LANES - 1
    turn_lo, turn_hi = pltpu.roll(code_lo, LANES - 1, 1), pltpu.roll(code_hi, LANES - 1, 1)
    next_lo = jnp.where(last_lane, turn_hi, turn_lo)
    next_hi = jnp.where(last_lane, code_hi, turn_hi)
    for half, (a, b) in enumerate(((code_lo, next_lo), (code_hi, next_hi))):
        word = a.astype(I32) | (b.astype(I32) << 16)
        for c in range(4):
            words[2 * c + half] = jnp.broadcast_to(word[c : c + 1], (8, LANES))

    band[...] = band_matrix()
    step = iota((XH, 2 * LANES), 1) % LANES - iota((XH, 2 * LANES), 0)
    pair[...] = choose((step >= 0) & (step <= 1), SCALE)

    load_entry.wait()
    even, odd = halves(ebuf[0:XH, :], ebuf[XH:XB, :], low)
    ent[...] = jnp.where(lax.rem(me, 2) == 0, even, odd)

    is_edge = (iota((8, LANES), 1) & (YB - 1)) == YB - 1
    row8 = iota((TILE, LANES), 0)
    zero = jnp.zeros((8, LANES), F32)
    one = jnp.ones((8, LANES), F32)
    gap = jnp.zeros((YB - TILE, 2 * LANES), F32)

    def arrived(d):
        pltpu.make_async_copy(rb.at[d], rb.at[d], mrecv.at[d]).wait()

        @pl.when(has_right)
        def _():
            pltpu.make_async_copy(cb.at[d], cb.at[d], crecv.at[d]).wait()

    def tile(d):
        return rb[d, BODY:ROWS, :].astype(F32) + cb[d].astype(F32)

    def lookup(scaled):
        lower = jnp.minimum(jnp.floor(scaled), 254.0)
        frac = scaled - lower
        index = lower.astype(I32)
        high = index >= LANES
        within = index & (LANES - 1)
        values = []
        for c in range(4):
            got = [jnp.take_along_axis(words[2 * c + p], within, axis=1, mode="promise_in_bounds") for p in range(2)]
            word = jnp.where(high, got[1], got[0])
            a = (word & 65535).astype(F32)
            b = lax.shift_right_logical(word, jnp.full_like(word, 16)).astype(F32)
            a = a * a
            b = b * b
            values.append(a + frac * (b - a))
        return values

    def brick(d, carry):
        cum, bright, acc = carry
        cum, bright = list(cum), list(bright)
        acc = [list(a) for a in acc]

        @pl.when(d < ND - 1)
        def _():
            arrived(d + 1)

        here, after = tile(d), tile(d + 1)
        data = jnp.concatenate(
            [rb[d, 0:BODY, :], rb[d + 1, 0:XH, :], jnp.concatenate([here, after], 0).astype(BF16)], 0
        )
        s = nn_dot(band[...], data)
        below = jnp.where(row8 == ZB - 1, jnp.broadcast_to(after[0:1], (TILE, LANES)), pltpu.roll(here, TILE - 1, 0))
        two = jnp.concatenate([here, below], 1)
        two_right = jnp.concatenate([pltpu.roll(here, LANES - XH, 1), pltpu.roll(below, LANES - XH, 1)], 1)
        edge = nt_dot(pair[...], jnp.concatenate([two, gap, two_right, gap], 0).astype(BF16))
        for z in range(ZB):
            for t in range(XT):
                value = s[XH * z + 8 * t : XH * z + 8 * t + 8]
                beyond = pltpu.roll(edge[8 * t : 8 * t + 8], YB - 1 - z, 1)
                colour = lookup(value + jnp.where(is_edge, beyond, pltpu.roll(value, LANES - 1, 1)))
                inside = ent[8 * t : 8 * t + 8, :] <= ZB * d + z
                cum[t] = cum[t] + jnp.where(inside, colour[3], 0.0)
                bright_next = jnp.exp2(cum[t] * OPTICAL)
                weight = bright[t] - bright_next
                bright[t] = bright_next
                for c in range(3):
                    acc[c][t] = acc[c][t] + weight * colour[c]
        return tuple(cum), tuple(bright), tuple(tuple(a) for a in acc)

    arrived(0)
    start = ((zero,) * XT, (one,) * XT, ((zero,) * XT,) * 3)
    _, bright, acc = lax.fori_loop(0, ND, brick, start)
    planes = jnp.concatenate([v * (UNIT * UNIT) for a in acc for v in a] + list(bright), 0)
    turned = planes.T
    for c in range(4):
        for h in range(2):
            out[c, :, XH * h : XH * (h + 1)] = turned[YB * h : YB * (h + 1), XH * c : XH * (c + 1)]

    sent = pk.at[pl.ds(0, ND - 1), pl.ds(0, BODY), :]
    pltpu.make_async_copy(sent, sent, msend).wait()
    tiles = pk.at[pl.ds(0, ND - 1), pl.ds(BODY, TILE), :]
    pltpu.make_async_copy(tiles, tiles, hsend).wait()

    @pl.when(has_left)
    def _():
        pltpu.make_async_copy(ck, ck, csend).wait()


def shards(volume, entry_depth, tf_table):
    dma = pltpu.SemaphoreType.DMA
    return pl.pallas_call(
        kernel,
        out_shape=jax.ShapeDtypeStruct((4, YB, XB), F32),
        in_specs=[
            pl.BlockSpec(memory_space=pl.ANY),
            pl.BlockSpec(memory_space=pl.ANY),
            pl.BlockSpec(memory_space=pltpu.VMEM),
        ],
        out_specs=pl.BlockSpec(memory_space=pltpu.VMEM),
        scratch_shapes=[
            pltpu.VMEM((ZB, XB, NY), BF16),
            pltpu.VMEM((XB, LANES), I32),
            pltpu.VMEM((ND, ROWS, LANES), BF16),
            pltpu.VMEM((ND, TILE, LANES), BF16),
            pltpu.VMEM((ND + 1, ROWS, LANES), BF16),
            pltpu.VMEM((ND + 1, TILE, LANES), BF16),
            pltpu.VMEM((8, 8, LANES), I32),
            pltpu.VMEM((XH, LANES), I32),
            pltpu.VMEM((BODY, KROWS), BF16),
            pltpu.VMEM((XH, 2 * LANES), BF16),
            dma, dma, dma, dma, dma,
            dma((ND,)), dma((ND,)),
        ],
        compiler_params=pltpu.CompilerParams(collective_id=0, has_side_effects=True),
        name="render",
    )(volume, entry_depth, tf_table.T)


def solution(mesh):
    placed = (P("depth", "img", None), P("img", None), P())
    return jax.shard_map(
        shards, mesh=mesh, in_specs=placed, out_specs=P(None, "depth", "img"), check_vma=False
    )
```

```python
import math

import jax
import jax.numpy as jnp
from jax import lax
from jax.experimental import pallas as pl
from jax.experimental.pallas import tpu as pltpu
from jax.sharding import PartitionSpec as P

MESH = pl.DeviceIdType.MESH
F32, BF16, I32 = jnp.float32, jnp.bfloat16, jnp.int32
ND = 16
NI = 16
ZB = 4
XB = 64
XH = 32
YB = 64
NY = ND * YB
LANES = 128
TILE = 8
BODY = ZB * XH
ROWS = BODY + TILE
KROWS = BODY + XH + 2 * TILE
XT = XH // 8
SCALE = 255.0 / 8.0
UNIT = 2.0 / 65535.0
OPTICAL = -2.0 / (ND * ZB) * math.log2(math.e) * UNIT * UNIT
EARLY = 2


def iota(shape, axis):
    return lax.broadcasted_iota(I32, shape, axis)


def choose(mask, value=1.0):
    return jnp.where(mask, value, 0.0).astype(BF16)


def nt_dot(a, b):
    return lax.dot_general(a, b, (((1,), (1,)), ((), ())), preferred_element_type=F32)


def nn_dot(a, b):
    return jnp.dot(a, b, preferred_element_type=F32)


def halves(a, b, low):
    turned = pltpu.roll(jnp.where(low, b, a), YB, 1)
    return jnp.where(low, a, turned), jnp.where(low, turned, b)


def band_matrix():
    row = iota((BODY, KROWS), 0)
    col = iota((BODY, KROWS), 1)
    z, x = row // XH, row % XH
    tile = col - (BODY + XH)
    in_tile = tile >= 0
    part = tile % TILE - ZB
    zz = jnp.where(in_tile, jnp.where(tile >= TILE, ZB + part, part), col // XH)
    used = (tile < 0) | ((tile < TILE) & (part >= 0)) | ((tile >= TILE) & (part == 0))
    xx = jnp.where(in_tile, XH, col % XH)
    dz, dx = zz - z, xx - x
    near = (dz >= 0) & (dz <= 1) & (dx >= 0) & (dx <= 1)
    return choose(near & used, SCALE)


def kernel(
    vol, entry, table, out,
    vbuf, ebuf, pk, ck, rb, cb, words, ent, band, pair, state, behind, sbuf,
    vsem, esem, msend, hsend, csend, mrecv, crecv,
):
    me = lax.axis_index("depth")
    im = lax.axis_index("img")
    base = me & (ND - 2)
    left = jnp.maximum(im - 1, 0)
    right = jnp.minimum(im + 1, NI - 1)
    has_left, has_right = im > 0, im < NI - 1

    load_vol = pltpu.make_async_copy(vol, vbuf, vsem)
    load_vol.start()
    group = pl.multiple_of((me // 2) * LANES, LANES)
    load_entry = pltpu.make_async_copy(entry.at[:, pl.ds(group, LANES)], ebuf, esem)
    load_entry.start()

    barrier = pltpu.get_barrier_semaphore()
    for k in range(1, ND):
        pl.semaphore_signal(barrier, 1, device_id={"img": im, "depth": me ^ k}, device_id_type=MESH)

    @pl.when(has_right)
    def _():
        for k in range(ND):
            pl.semaphore_signal(barrier, 1, device_id={"img": right, "depth": me ^ k}, device_id_type=MESH)

    low = iota((XH, LANES), 1) < YB
    low8 = iota((TILE, LANES), 1) < YB

    load_vol.wait()
    for g in range(ND // 2):
        lanes = slice(LANES * g, LANES * (g + 1))
        for z in range(ZB):
            a, b = halves(vbuf[z, 0:XH, lanes], vbuf[z, XH:XB, lanes], low)
            pk[2 * g, XH * z : XH * (z + 1), :] = a
            pk[2 * g + 1, XH * z : XH * (z + 1), :] = b

    pl.semaphore_wait(barrier, jnp.where(has_left, 2 * ND - 1, ND - 1))

    def target_of(step):
        return (me ^ 1) if step == 0 else (base - step // 2 * 2 + step % 2) & (ND - 1)

    def send(step, first, rows, sem):
        target = target_of(step)
        return pltpu.make_async_remote_copy(
            pk.at[target, pl.ds(first, rows), :], rb.at[me, pl.ds(first, rows), :], sem, mrecv.at[me],
            device_id={"img": im, "depth": target}, device_id_type=MESH,
        )

    steps = [0] + list(range(2, ND))
    for step in steps[:EARLY]:
        send(step, 0, BODY, hsend).start()

    sel = choose(iota((ND, NY), 1) == iota((ND, NY), 0) * YB + YB)
    zero_row = jnp.zeros((1, NY), F32)
    pad = jnp.zeros((ND, LANES - XB), F32)
    by_row = [jnp.concatenate([nt_dot(sel, vbuf[z]), pad], 1) for z in range(ZB)]
    spot = iota((LANES, ZB * ND), 0)
    block = iota((LANES, ZB * ND), 1)
    place = choose((spot // TILE == block % ND) & (spot % TILE == block // ND))
    mine = nn_dot(place, jnp.concatenate(by_row, 0).astype(BF16))
    middle = jnp.concatenate([zero_row] * 4 + [vbuf[z, XH : XH + 1, :].astype(F32) for z in range(ZB)], 0)
    for g in range(ND // 2):
        a = middle[:, LANES * g : LANES * (g + 1)]
        turned = pltpu.roll(a, YB, 1)
        at = 2 * TILE * g
        pk[2 * g, BODY:ROWS, :] = (mine[at : at + TILE] + jnp.where(low8, a, 0.0)).astype(BF16)
        pk[2 * g + 1, BODY:ROWS, :] = (mine[at + TILE : at + 2 * TILE] + jnp.where(low8, turned, 0.0)).astype(BF16)

    for step in steps[:EARLY]:
        send(step, BODY, TILE, hsend).start()
    for step in steps[EARLY:]:
        send(step, 0, ROWS, msend).start()
    pltpu.make_async_copy(pk.at[me], rb.at[me], mrecv.at[me]).start()

    first = jnp.concatenate([vbuf[z, 0:1, :].astype(F32) for z in range(ZB)] + [zero_row] * 4, 0)
    corner = nt_dot(sel, first.astype(BF16)).astype(BF16)
    spot16 = iota((LANES, ND), 0)
    spread = nn_dot(choose(spot16 // TILE == iota((LANES, ND), 1)), corner)
    lane8 = iota((LANES, TILE), 1)
    spread = jnp.sum(jnp.where(lane8 == iota((LANES, TILE), 0) % TILE, spread, 0.0), 1, keepdims=True)
    lane = iota((LANES, LANES), 1)
    at_corner = jnp.where((lane == YB) & (iota((LANES, LANES), 0) % TILE < ZB), jnp.broadcast_to(spread, (LANES, LANES)), 0.0)
    first = pltpu.roll(first, 4, 0)
    for g in range(ND // 2):
        a = first[:, LANES * g : LANES * (g + 1)]
        turned = pltpu.roll(a, YB, 1)
        at = 2 * TILE * g
        ck[2 * g] = (at_corner[at : at + TILE] + jnp.where(low8, 0.0, turned)).astype(BF16)
        ck[2 * g + 1] = (at_corner[at + TILE : at + 2 * TILE] + jnp.where(low8, 0.0, a)).astype(BF16)

    @pl.when(has_left)
    def _():
        for step in range(ND):
            target = (base - step // 2 * 2 + step % 2) & (ND - 1)
            pltpu.make_async_remote_copy(
                ck.at[target], cb.at[me], csend, crecv.at[me],
                device_id={"img": left, "depth": target}, device_id_type=MESH,
            ).start()

    rb[ND] = jnp.zeros((ROWS, LANES), BF16)
    cb[ND] = jnp.zeros((TILE, LANES), BF16)

    @pl.when(jnp.logical_not(has_right))
    def _():
        cb[0:ND] = jnp.zeros((ND, TILE, LANES), BF16)

    code = jnp.floor(jnp.sqrt(table[...]) * (1.0 / UNIT) + 0.5)
    code = jnp.concatenate([code, code], 0).astype(I32)
    lane128 = iota((8, LANES), 1)
    even_of = (2 * lane128) & (LANES - 1)

    def every_other(offset):
        lo, hi = (
            jnp.take_along_axis(part, even_of + offset, axis=1, mode="promise_in_bounds")
            for part in (code[:, :LANES], code[:, LANES:])
        )
        return jnp.where(lane128 < LANES // 2, lo, hi)

    even_code, odd_code = every_other(0), every_other(1)
    next_code = pltpu.roll(even_code, LANES - 1, 1)
    for c in range(4):
        words[c] = jnp.broadcast_to((even_code | (odd_code << 16))[c : c + 1], (8, LANES))
    for p in range(2):
        word = next_code[2 * p : 2 * p + 1] | (next_code[2 * p + 1 : 2 * p + 2] << 16)
        words[4 + p] = jnp.broadcast_to(word, (8, LANES))

    band[...] = band_matrix()
    step = iota((XH, 2 * LANES), 1) % LANES - iota((XH, 2 * LANES), 0)
    pair[...] = choose((step >= 0) & (step <= 1), SCALE)

    load_entry.wait()
    even, odd = halves(ebuf[0:XH, :], ebuf[XH:XB, :], low)
    ent[...] = jnp.where(lax.rem(me, 2) == 0, even, odd)

    is_edge = (iota((8, LANES), 1) & (YB - 1)) == YB - 1
    row8 = iota((TILE, LANES), 0)
    zero = jnp.zeros((8, LANES), F32)
    one = jnp.ones((8, LANES), F32)
    gap = jnp.zeros((YB - TILE, 2 * LANES), F32)

    def arrived(d):
        pltpu.make_async_copy(rb.at[d], rb.at[d], mrecv.at[d]).wait()

        @pl.when(has_right)
        def _():
            pltpu.make_async_copy(cb.at[d], cb.at[d], crecv.at[d]).wait()

    def tile(d):
        return rb[d, BODY:ROWS, :].astype(F32) + cb[d].astype(F32)

    def lookup(scaled):
        lower = jnp.minimum(jnp.floor(scaled), 254.0)
        frac = scaled - lower
        index = lower.astype(I32)
        odd = (index & 1) == 1
        within = lax.shift_right_logical(index, jnp.full_like(index, 1))

        def get(i):
            return jnp.take_along_axis(words[i], within, axis=1, mode="promise_in_bounds")

        values = []
        beyond = (get(4), get(5))
        for c in range(4):
            word = get(c)
            a = word & 65535
            b = lax.shift_right_logical(word, jnp.full_like(word, 16))
            e = beyond[c // 2]
            e = lax.shift_right_logical(e, jnp.full_like(e, 16)) if c % 2 else e & 65535
            lo = jnp.where(odd, b, a).astype(F32)
            hi = jnp.where(odd, e, b).astype(F32)
            lo = lo * lo
            hi = hi * hi
            values.append(lo + frac * (hi - lo))
        return values

    def sums(d):
        here, after = tile(d), tile(d + 1)
        data = jnp.concatenate(
            [rb[d, 0:BODY, :], rb[d + 1, 0:XH, :], jnp.concatenate([here, after], 0).astype(BF16)], 0
        )
        below = jnp.where(row8 == ZB - 1, jnp.broadcast_to(after[0:1], (TILE, LANES)), pltpu.roll(here, TILE - 1, 0))
        two = jnp.concatenate([here, below], 1)
        two_right = jnp.concatenate([pltpu.roll(here, LANES - XH, 1), pltpu.roll(below, LANES - XH, 1)], 1)
        edge = nt_dot(pair[...], jnp.concatenate([two, gap, two_right, gap], 0).astype(BF16))
        s = nn_dot(band[...], data)
        for z in range(ZB):
            for t in range(XT):
                value = s[XH * z + 8 * t : XH * z + 8 * t + 8]
                beyond = pltpu.roll(edge[8 * t : 8 * t + 8], YB - 1 - z, 1)
                sbuf[d, XH * z + 8 * t : XH * z + 8 * t + 8, :] = value + jnp.where(is_edge, beyond, pltpu.roll(value, LANES - 1, 1))

    def render(d, cum, bright, acc):
        for z in range(ZB):
            for t in range(XT):
                colour = lookup(sbuf[d, XH * z + 8 * t : XH * z + 8 * t + 8, :])
                inside = ent[8 * t : 8 * t + 8, :] <= ZB * d + z
                cum[t] = cum[t] + jnp.where(inside, colour[3], 0.0)
                bright_next = jnp.exp2(cum[t] * OPTICAL)
                weight = bright[t] - bright_next
                bright[t] = bright_next
                for c in range(3):
                    acc[c][t] = acc[c][t] + weight * colour[c]

    def fresh():
        for i in range(5 * XT):
            state[i] = one if XT <= i < 2 * XT else zero

    def two_bricks(i, _):
        d = (base + 2 * i) & (ND - 1)
        arrived(d + 1)

        @pl.when(i < ND // 2 - 1)
        def _():
            arrived((d + 2) & (ND - 1))

        @pl.when(d == 0)
        def _():
            behind[...] = state[...]
            fresh()

        sums(d)
        sums(d + 1)
        cum = [state[t] for t in range(XT)]
        bright = [state[XT + t] for t in range(XT)]
        acc = [[state[(2 + c) * XT + t] for t in range(XT)] for c in range(3)]
        render(d, cum, bright, acc)
        render(d + 1, cum, bright, acc)
        for i, v in enumerate(cum + bright + [v for a in acc for v in a]):
            state[i] = v
        return 0

    fresh()
    arrived(base)
    lax.fori_loop(0, ND // 2, two_bricks, 0)
    bright = [state[XT + t] * behind[XT + t] for t in range(XT)]
    acc = [
        [state[(2 + c) * XT + t] + state[XT + t] * behind[(2 + c) * XT + t] for t in range(XT)] for c in range(3)
    ]
    planes = jnp.concatenate([v * (UNIT * UNIT) for a in acc for v in a] + list(bright), 0)
    turned = planes.T
    for c in range(4):
        for h in range(2):
            out[c, :, XH * h : XH * (h + 1)] = turned[YB * h : YB * (h + 1), XH * c : XH * (c + 1)]

    early = pk.at[pl.ds(0, EARLY)]
    pltpu.make_async_copy(early, early, hsend).wait()
    rest = pk.at[pl.ds(0, ND - 1 - EARLY)]
    pltpu.make_async_copy(rest, rest, msend).wait()

    @pl.when(has_left)
    def _():
        pltpu.make_async_copy(ck, ck, csend).wait()


def shards(volume, entry_depth, tf_table):
    dma = pltpu.SemaphoreType.DMA
    return pl.pallas_call(
        kernel,
        out_shape=jax.ShapeDtypeStruct((4, YB, XB), F32),
        in_specs=[
            pl.BlockSpec(memory_space=pl.ANY),
            pl.BlockSpec(memory_space=pl.ANY),
            pl.BlockSpec(memory_space=pltpu.VMEM),
        ],
        out_specs=pl.BlockSpec(memory_space=pltpu.VMEM),
        scratch_shapes=[
            pltpu.VMEM((ZB, XB, NY), BF16),
            pltpu.VMEM((XB, LANES), I32),
            pltpu.VMEM((ND, ROWS, LANES), BF16),
            pltpu.VMEM((ND, TILE, LANES), BF16),
            pltpu.VMEM((ND + 1, ROWS, LANES), BF16),
            pltpu.VMEM((ND + 1, TILE, LANES), BF16),
            pltpu.VMEM((8, 8, LANES), I32),
            pltpu.VMEM((XH, LANES), I32),
            pltpu.VMEM((BODY, KROWS), BF16),
            pltpu.VMEM((XH, 2 * LANES), BF16),
            pltpu.VMEM((5 * XT, 8, LANES), F32),
            pltpu.VMEM((5 * XT, 8, LANES), F32),
            pltpu.VMEM((ND, BODY, LANES), F32),
            dma, dma, dma, dma, dma,
            dma((ND,)), dma((ND,)),
        ],
        compiler_params=pltpu.CompilerParams(collective_id=0, has_side_effects=True),
        name="render",
    )(volume, entry_depth, tf_table.T)


def solution(mesh):
    placed = (P("depth", "img", None), P("img", None), P())
    return jax.shard_map(
        shards, mesh=mesh, in_specs=placed, out_specs=P(None, "depth", "img"), check_vma=False
    )
```

```python
import math

import jax
import jax.numpy as jnp
from jax import lax
from jax.experimental import pallas as pl
from jax.experimental.pallas import tpu as pltpu
from jax.sharding import PartitionSpec as P

MESH = pl.DeviceIdType.MESH
F32, BF16, I32 = jnp.float32, jnp.bfloat16, jnp.int32
ND = 16
NI = 16
ZB = 4
NZ = ND * ZB
XB = 64
XH = 32
XT = 8
NC = XH // XT
YB = 64
NY = ND * YB
LANES = 128
TILE = 8
CHUNK = ZB * XT
GROUP = 8
DEPTH = GROUP * XT + 2 * XT
SCALE = 255.0 / 8.0
UNIT = 2.0 / 65535.0
OPTICAL = -2.0 / NZ * math.log2(math.e) * UNIT * UNIT
PLANES = 32


def iota(shape, axis):
    return lax.broadcasted_iota(I32, shape, axis)


def choose(mask, value=1.0):
    return jnp.where(mask, value, 0.0).astype(BF16)


def nt_dot(a, b):
    return lax.dot_general(a, b, (((1,), (1,)), ((), ())), preferred_element_type=F32)


def nn_dot(a, b):
    return jnp.dot(a, b, preferred_element_type=F32)


def halves(a, b, low):
    turned = pltpu.roll(jnp.where(low, b, a), YB, 1)
    return jnp.where(low, a, turned), jnp.where(low, turned, b)


def band_matrix():
    row = iota((GROUP * XT, 2 * DEPTH), 0)
    col = iota((GROUP * XT, 2 * DEPTH), 1)
    second = col >= DEPTH
    local = jnp.where(second, col - DEPTH, col)
    dz = local // XT - row // XT
    dx = jnp.where(second, XT, 0) + local % XT - row % XT
    return choose((dz >= 0) & (dz <= 1) & (dx >= 0) & (dx <= 1), SCALE)


def kernel(
    vol, entry, table, out,
    vbuf, ebuf, pk, hk, ck, rb, hb, cb, hcb, words, ent, band, edges, sbuf, result,
    vsem, esem, bsend, hsend, csend, brecv, hrecv, crecv,
):
    me = lax.axis_index("depth")
    im = lax.axis_index("img")
    left = jnp.maximum(im - 1, 0)
    right = jnp.minimum(im + 1, NI - 1)
    has_left, has_right = im > 0, im < NI - 1

    def load(part, first):
        rows = pl.ds(first, 2 * XT)
        return pltpu.make_async_copy(vol.at[:, rows, :], vbuf.at[:, rows, :], vsem.at[part])

    firsts = (2 * XT, XH + 2 * XT, 0, XH)
    for part, first in enumerate(firsts):
        load(part, first).start()
    group = pl.multiple_of((me // 2) * LANES, LANES)
    load_entry = pltpu.make_async_copy(entry.at[:, pl.ds(group, LANES)], ebuf, esem)
    load_entry.start()

    barrier = pltpu.get_barrier_semaphore()
    for k in range(1, ND):
        pl.semaphore_signal(barrier, 1, device_id={"img": im, "depth": me ^ k}, device_id_type=MESH)

    @pl.when(has_right)
    def _():
        for k in range(ND):
            pl.semaphore_signal(barrier, 1, device_id={"img": right, "depth": me ^ k}, device_id_type=MESH)

    low = iota((2 * XT, LANES), 1) < YB
    low8 = iota((TILE, LANES), 1) < YB

    def pack(first_chunk):
        x = XT * first_chunk
        for g in range(ND // 2):
            lanes = slice(LANES * g, LANES * (g + 1))
            for z in range(ZB):
                pair = halves(vbuf[z, x : x + 2 * XT, lanes], vbuf[z, XH + x : XH + x + 2 * XT, lanes], low)
                for odd, v in enumerate(pair):
                    for c in range(2):
                        pk[(first_chunk + c) * ND + 2 * g + odd, XT * z : XT * (z + 1), :] = v[XT * c : XT * (c + 1)]

    def send_chunk(c):
        here = pl.ds(pl.multiple_of(CHUNK * me, CHUNK), CHUNK)
        for k in range(1, ND):
            pltpu.make_async_remote_copy(
                pk.at[c * ND + (me ^ k)], rb.at[c, here, :], bsend, brecv.at[c],
                device_id={"img": im, "depth": me ^ k}, device_id_type=MESH,
            ).start()
        pltpu.make_async_copy(pk.at[c * ND + me], rb.at[c, here, :], brecv.at[c]).start()

    load(0, firsts[0]).wait()
    load(1, firsts[1]).wait()
    pack(2)
    pl.semaphore_wait(barrier, jnp.where(has_left, 2 * ND - 1, ND - 1))
    send_chunk(3)

    load(2, firsts[2]).wait()
    load(3, firsts[3]).wait()
    sel = choose(iota((ND, NY), 1) == iota((ND, NY), 0) * YB + YB)
    zero_row = jnp.zeros((1, NY), F32)
    pad = jnp.zeros((ND, LANES - XB), F32)
    by_row = [jnp.concatenate([nt_dot(sel, vbuf[z]), pad], 1) for z in range(ZB)]
    first = jnp.concatenate([vbuf[z, 0:1, :].astype(F32) for z in range(ZB)] + [zero_row] * 4, 0)
    corner = nt_dot(sel, first.astype(BF16)).astype(BF16)
    spot = iota((LANES, ZB * ND), 0)
    block = iota((LANES, ZB * ND), 1)
    place = choose((spot // TILE == block % ND) & (spot % TILE == block // ND))
    mine = nn_dot(place, jnp.concatenate(by_row, 0).astype(BF16))
    spot16 = iota((LANES, ND), 0)
    spread = nn_dot(choose(spot16 // TILE == iota((LANES, ND), 1)), corner)
    lane8 = iota((LANES, TILE), 1)
    spread = jnp.sum(jnp.where(lane8 == iota((LANES, TILE), 0) % TILE, spread, 0.0), 1, keepdims=True)
    lane = iota((LANES, LANES), 1)
    at_corner = jnp.where((lane == YB) & (iota((LANES, LANES), 0) % TILE < ZB), jnp.broadcast_to(spread, (LANES, LANES)), 0.0)
    middle = jnp.concatenate([zero_row] * 4 + [vbuf[z, XH : XH + 1, :].astype(F32) for z in range(ZB)], 0)
    first = jnp.concatenate([zero_row] * 4 + [vbuf[z, 0:1, :].astype(F32) for z in range(ZB)], 0)
    for g in range(ND // 2):
        lanes = slice(LANES * g, LANES * (g + 1))
        a, b = middle[:, lanes], first[:, lanes]
        turned = pltpu.roll(jnp.where(low8, b, a), YB, 1)
        at = 2 * TILE * g
        hk[2 * g] = (mine[at : at + TILE] + jnp.where(low8, a, 0.0)).astype(BF16)
        hk[2 * g + 1] = (mine[at + TILE : at + 2 * TILE] + jnp.where(low8, turned, 0.0)).astype(BF16)
        ck[2 * g] = (at_corner[at : at + TILE] + jnp.where(low8, 0.0, turned)).astype(BF16)
        ck[2 * g + 1] = (at_corner[at + TILE : at + 2 * TILE] + jnp.where(low8, 0.0, b)).astype(BF16)

    tile_here = pl.ds(pl.multiple_of(TILE * me, TILE), TILE)
    for k in range(1, ND):
        pltpu.make_async_remote_copy(
            hk.at[me ^ k], hb.at[tile_here, :], hsend, hrecv,
            device_id={"img": im, "depth": me ^ k}, device_id_type=MESH,
        ).start()
    pltpu.make_async_copy(hk.at[me], hb.at[tile_here, :], hrecv).start()

    @pl.when(has_left)
    def _():
        for k in range(ND):
            pltpu.make_async_remote_copy(
                ck.at[me ^ k], cb.at[tile_here, :], csend, crecv,
                device_id={"img": left, "depth": me ^ k}, device_id_type=MESH,
            ).start()

    send_chunk(2)
    pack(0)
    send_chunk(1)
    send_chunk(0)

    for c in range(NC + 1):
        rb[c, ND * CHUNK : (ND + 1) * CHUNK, :] = jnp.zeros((CHUNK, LANES), BF16)

    @pl.when(jnp.logical_not(has_right))
    def _():
        cb[...] = jnp.zeros((ND * TILE, LANES), BF16)

    code = jnp.floor(jnp.sqrt(table[...]) * (1.0 / UNIT) + 0.5)
    code = jnp.concatenate([code, code], 0).astype(I32)
    lane128 = iota((8, LANES), 1)
    even_of = (2 * lane128) & (LANES - 1)

    def every_other(offset):
        lo, hi = (
            jnp.take_along_axis(part, even_of + offset, axis=1, mode="promise_in_bounds")
            for part in (code[:, :LANES], code[:, LANES:])
        )
        return jnp.where(lane128 < LANES // 2, lo, hi)

    even_code, odd_code = every_other(0), every_other(1)
    next_code = pltpu.roll(even_code, LANES - 1, 1)
    for c in range(4):
        words[c] = jnp.broadcast_to((even_code | (odd_code << 16))[c : c + 1], (8, LANES))
    for p in range(2):
        word = next_code[2 * p : 2 * p + 1] | (next_code[2 * p + 1 : 2 * p + 2] << 16)
        words[4 + p] = jnp.broadcast_to(word, (8, LANES))

    band[...] = band_matrix()

    load_entry.wait()
    low32 = iota((XH, LANES), 1) < YB
    even, odd = halves(ebuf[0:XH, :], ebuf[XH:XB, :], low32)
    ent[...] = jnp.where(lax.rem(me, 2) == 0, even, odd)

    is_edge = (iota((8, LANES), 1) & (YB - 1)) == YB - 1
    zero = jnp.zeros((8, LANES), F32)
    one = jnp.ones((8, LANES), F32)

    def make_edges(tiles):
        x = iota((XB, LANES), 0)
        dx = iota((XB, LANES), 1) - x
        sums = nt_dot(choose((dx >= 0) & (dx <= 1), SCALE), tiles)
        lane = iota((XB, LANES), 1)
        after = jnp.where(
            lane % TILE == ZB - 1,
            jnp.where(lane >= LANES - TILE, 0.0, pltpu.roll(sums, LANES - TILE + ZB - 1, 1)),
            pltpu.roll(sums, LANES - 1, 1),
        )
        sums += after
        front, back = halves(sums[:XH], sums[XH:], low32)
        edges[0] = front
        edges[1] = back

    def lookup(scaled):
        lower = jnp.minimum(jnp.floor(scaled), 254.0)
        frac = scaled - lower
        index = lower.astype(I32)
        odd = (index & 1) == 1
        within = lax.shift_right_logical(index, jnp.full_like(index, 1))

        def get(i):
            return jnp.take_along_axis(words[i], within, axis=1, mode="promise_in_bounds")

        values = []
        beyond = (get(4), get(5))
        for c in range(4):
            word = get(c)
            a = word & 65535
            b = lax.shift_right_logical(word, jnp.full_like(word, 16))
            e = beyond[c // 2]
            e = lax.shift_right_logical(e, jnp.full_like(e, 16)) if c % 2 else e & 65535
            lo = jnp.where(odd, b, a).astype(F32)
            hi = jnp.where(odd, e, b).astype(F32)
            lo = lo * lo
            hi = hi * hi
            values.append(lo + frac * (hi - lo))
        return values

    def wait_chunk(c):
        here = rb.at[c, pl.ds(0, ND * CHUNK), :]
        pltpu.make_async_copy(here, here, brecv.at[c]).wait()

    def column_tile(o, _):
        t = jnp.where(o == 0, 2, jnp.where(o == 1, 1, jnp.where(o == 2, 3, 0)))

        @pl.when(o == 0)
        def _():
            wait_chunk(3)
            wait_chunk(2)
            pltpu.make_async_copy(hb, hb, hrecv).wait()
            make_edges(hb[...])

        @pl.when(o == 1)
        def _():
            wait_chunk(1)

        @pl.when(o == 2)
        def _():
            @pl.when(has_right)
            def _():
                pltpu.make_async_copy(cb, cb, crecv).wait()

            hcb[...] = (hb[...].astype(F32) + cb[...].astype(F32)).astype(BF16)
            make_edges(hcb[...])
            n = ND // 2
            row = iota((n * CHUNK, n * TILE), 0)
            src = iota((n * CHUNK, n * TILE), 1)
            grow = choose((row // CHUNK == src // TILE) & (row % XT == 0) & (src % TILE == ZB + row // XT % ZB))
            for p in range(2):
                rows = nn_dot(grow, hcb[p * n * TILE : (p + 1) * n * TILE, :])
                rb[NC, p * n * CHUNK : (p + 1) * n * CHUNK, :] = rows.astype(BF16)

        @pl.when(o == 3)
        def _():
            wait_chunk(0)

        cols = pl.ds(pl.multiple_of(XT * t, XT), XT)
        for g in range(NZ // GROUP):
            at = GROUP * XT * g
            data = jnp.concatenate([rb[t, at : at + DEPTH, :], rb[t + 1, at : at + DEPTH, :]], 0)
            s = nn_dot(band[...], data)
            for z in range(GROUP):
                plane = GROUP * g + z
                d, r = plane // ZB, plane % ZB
                value = s[XT * z : XT * (z + 1)]
                beyond = pltpu.roll(edges[d // 8, cols, :], (YB - 1 - TILE * (d % 8) - r) % LANES, 1)
                sbuf[plane] = value + jnp.where(is_edge, beyond, pltpu.roll(value, LANES - 1, 1))

        entry_here = ent[cols, :]

        def planes(i, carry):
            cum, bright, acc = carry
            acc = list(acc)
            for p in range(PLANES):
                plane = PLANES * i + p
                colour = lookup(sbuf[plane])
                cum = cum + jnp.where(entry_here <= plane, colour[3], 0.0)
                bright_next = jnp.exp2(cum * OPTICAL)
                weight = bright - bright_next
                bright = bright_next
                for c in range(3):
                    acc[c] = acc[c] + weight * colour[c]
            return cum, bright, tuple(acc)

        _, bright, acc = lax.fori_loop(0, NZ // PLANES, planes, (zero, one, (zero,) * 3))
        for c in range(3):
            result[c, cols, :] = acc[c] * (UNIT * UNIT)
        result[3, cols, :] = bright
        return 0

    lax.fori_loop(0, NC, column_tile, 0)
    turned = result[...].reshape(4 * XH, LANES).T
    for c in range(4):
        for h in range(2):
            out[c, :, XH * h : XH * (h + 1)] = turned[YB * h : YB * (h + 1), XH * c : XH * (c + 1)]

    sent = pk.at[pl.ds(0, NC * (ND - 1))]
    pltpu.make_async_copy(sent, sent, bsend).wait()
    tiles = hk.at[pl.ds(0, ND - 1)]
    pltpu.make_async_copy(tiles, tiles, hsend).wait()

    @pl.when(has_left)
    def _():
        pltpu.make_async_copy(ck, ck, csend).wait()


def shards(volume, entry_depth, tf_table):
    dma = pltpu.SemaphoreType.DMA
    return pl.pallas_call(
        kernel,
        out_shape=jax.ShapeDtypeStruct((4, YB, XB), F32),
        in_specs=[
            pl.BlockSpec(memory_space=pl.ANY),
            pl.BlockSpec(memory_space=pl.ANY),
            pl.BlockSpec(memory_space=pltpu.VMEM),
        ],
        out_specs=pl.BlockSpec(memory_space=pltpu.VMEM),
        scratch_shapes=[
            pltpu.VMEM((ZB, XB, NY), BF16),
            pltpu.VMEM((XB, LANES), I32),
            pltpu.VMEM((NC * ND, CHUNK, LANES), BF16),
            pltpu.VMEM((ND, TILE, LANES), BF16),
            pltpu.VMEM((ND, TILE, LANES), BF16),
            pltpu.VMEM((NC + 1, (ND + 1) * CHUNK, LANES), BF16),
            pltpu.VMEM((ND * TILE, LANES), BF16),
            pltpu.VMEM((ND * TILE, LANES), BF16),
            pltpu.VMEM((ND * TILE, LANES), BF16),
            pltpu.VMEM((6, 8, LANES), I32),
            pltpu.VMEM((XH, LANES), I32),
            pltpu.VMEM((GROUP * XT, 2 * DEPTH), BF16),
            pltpu.VMEM((2, XH, LANES), F32),
            pltpu.VMEM((NZ, XT, LANES), F32),
            pltpu.VMEM((4, XH, LANES), F32),
            dma((4,)), dma, dma, dma, dma,
            dma((NC,)), dma, dma,
        ],
        compiler_params=pltpu.CompilerParams(collective_id=0, has_side_effects=True),
        name="render",
    )(volume, entry_depth, tf_table.T)


def solution(mesh):
    placed = (P("depth", "img", None), P("img", None), P())
    return jax.shard_map(
        shards, mesh=mesh, in_specs=placed, out_specs=P(None, "depth", "img"), check_vma=False
    )
```

```python
import math

import jax
import jax.numpy as jnp
from jax import lax
from jax.experimental import pallas as pl
from jax.experimental.pallas import tpu as pltpu
from jax.sharding import PartitionSpec as P

MESH = pl.DeviceIdType.MESH
F32, BF16, I32 = jnp.float32, jnp.bfloat16, jnp.int32
ND = 16
NI = 16
ZB = 4
NZ = ND * ZB
XB = 64
XH = 32
XT = 8
NC = XH // XT
YB = 64
NY = ND * YB
LANES = 128
TILE = 8
CHUNK = ZB * XT
GROUP = 8
DEPTH = GROUP * XT + 2 * XT
SCALE = 255.0 / 8.0
UNIT = 2.0 / 65535.0
OPTICAL = -2.0 / NZ * math.log2(math.e) * UNIT * UNIT
PLANES = 32
FAR_FIRST = sorted(range(1, ND), key=lambda k: -((0, 1, 2, 1)[k & 3] + (0, 1, 2, 1)[k >> 2]))


def iota(shape, axis):
    return lax.broadcasted_iota(I32, shape, axis)


def choose(mask, value=1.0):
    return jnp.where(mask, value, 0.0).astype(BF16)


def nt_dot(a, b):
    return lax.dot_general(a, b, (((1,), (1,)), ((), ())), preferred_element_type=F32)


def nn_dot(a, b):
    return jnp.dot(a, b, preferred_element_type=F32)


def halves(a, b, low):
    turned = pltpu.roll(jnp.where(low, b, a), YB, 1)
    return jnp.where(low, a, turned), jnp.where(low, turned, b)


def band_matrix():
    row = iota((GROUP * XT, 2 * DEPTH), 0)
    col = iota((GROUP * XT, 2 * DEPTH), 1)
    second = col >= DEPTH
    local = jnp.where(second, col - DEPTH, col)
    dz = local // XT - row // XT
    dx = jnp.where(second, XT, 0) + local % XT - row % XT
    return choose((dz >= 0) & (dz <= 1) & (dx >= 0) & (dx <= 1), SCALE)


def kernel(
    vol, entry, table, out,
    vbuf, ebuf, pk, hk, ck, rb, hb, cb, hcb, words, ent, band, edges, sbuf, result,
    vsem, esem, bsend, hsend, csend, brecv, hrecv, crecv, go,
):
    me = lax.axis_index("depth")
    im = lax.axis_index("img")
    left = jnp.maximum(im - 1, 0)
    right = jnp.minimum(im + 1, NI - 1)
    has_left, has_right = im > 0, im < NI - 1

    def load(part, first):
        rows = pl.ds(first, 2 * XT)
        return pltpu.make_async_copy(vol.at[:, rows, :], vbuf.at[:, rows, :], vsem.at[part])

    firsts = (2 * XT, XH + 2 * XT, 0, XH)
    for part, first in enumerate(firsts):
        load(part, first).start()
    group = pl.multiple_of((me // 2) * LANES, LANES)
    load_entry = pltpu.make_async_copy(entry.at[:, pl.ds(group, LANES)], ebuf, esem)
    load_entry.start()

    barrier = pltpu.get_barrier_semaphore()
    for k in FAR_FIRST:
        pl.semaphore_signal(barrier, 1, device_id={"img": im, "depth": me ^ k}, device_id_type=MESH)

    @pl.when(has_left)
    def _():
        pl.semaphore_signal(barrier, 1, device_id={"img": left, "depth": me}, device_id_type=MESH)

    low = iota((2 * XT, LANES), 1) < YB
    low8 = iota((TILE, LANES), 1) < YB

    def pack(first_chunk):
        x = XT * first_chunk
        for g in range(ND // 2):
            lanes = slice(LANES * g, LANES * (g + 1))
            for z in range(ZB):
                pair = halves(vbuf[z, x : x + 2 * XT, lanes], vbuf[z, XH + x : XH + x + 2 * XT, lanes], low)
                for odd, v in enumerate(pair):
                    for c in range(2):
                        pk[(first_chunk + c) * ND + 2 * g + odd, XT * z : XT * (z + 1), :] = v[XT * c : XT * (c + 1)]

    def send_chunk(c):
        here = pl.ds(pl.multiple_of(CHUNK * me, CHUNK), CHUNK)
        for k in FAR_FIRST:
            pltpu.make_async_remote_copy(
                pk.at[c * ND + (me ^ k)], rb.at[c, here, :], bsend, brecv.at[c],
                device_id={"img": im, "depth": me ^ k}, device_id_type=MESH,
            ).start()
        pltpu.make_async_copy(pk.at[c * ND + me], rb.at[c, here, :], brecv.at[c]).start()

    load(0, firsts[0]).wait()
    load(1, firsts[1]).wait()
    pack(2)
    pl.semaphore_wait(barrier, jnp.where(has_right, ND, ND - 1))

    @pl.when(has_right)
    def _():
        pl.semaphore_signal(go, 1, device_id={"img": right, "depth": me}, device_id_type=MESH)

    send_chunk(3)

    load(2, firsts[2]).wait()
    load(3, firsts[3]).wait()
    sel = choose(iota((ND, NY), 1) == iota((ND, NY), 0) * YB + YB)
    zero_row = jnp.zeros((1, NY), F32)
    pad = jnp.zeros((ND, LANES - XB), F32)
    by_row = [jnp.concatenate([nt_dot(sel, vbuf[z]), pad], 1) for z in range(ZB)]
    first = jnp.concatenate([vbuf[z, 0:1, :].astype(F32) for z in range(ZB)] + [zero_row] * 4, 0)
    corner = nt_dot(sel, first.astype(BF16)).astype(BF16)
    spot = iota((LANES, ZB * ND), 0)
    block = iota((LANES, ZB * ND), 1)
    place = choose((spot // TILE == block % ND) & (spot % TILE == block // ND))
    mine = nn_dot(place, jnp.concatenate(by_row, 0).astype(BF16))
    spot16 = iota((LANES, ND), 0)
    spread = nn_dot(choose(spot16 // TILE == iota((LANES, ND), 1)), corner)
    lane8 = iota((LANES, TILE), 1)
    spread = jnp.sum(jnp.where(lane8 == iota((LANES, TILE), 0) % TILE, spread, 0.0), 1, keepdims=True)
    lane = iota((LANES, LANES), 1)
    at_corner = jnp.where((lane == YB) & (iota((LANES, LANES), 0) % TILE < ZB), jnp.broadcast_to(spread, (LANES, LANES)), 0.0)
    middle = jnp.concatenate([zero_row] * 4 + [vbuf[z, XH : XH + 1, :].astype(F32) for z in range(ZB)], 0)
    first = jnp.concatenate([zero_row] * 4 + [vbuf[z, 0:1, :].astype(F32) for z in range(ZB)], 0)
    for g in range(ND // 2):
        lanes = slice(LANES * g, LANES * (g + 1))
        a, b = middle[:, lanes], first[:, lanes]
        turned = pltpu.roll(jnp.where(low8, b, a), YB, 1)
        at = 2 * TILE * g
        hk[2 * g] = (mine[at : at + TILE] + jnp.where(low8, a, 0.0)).astype(BF16)
        hk[2 * g + 1] = (mine[at + TILE : at + 2 * TILE] + jnp.where(low8, turned, 0.0)).astype(BF16)
        ck[2 * g] = (at_corner[at : at + TILE] + jnp.where(low8, 0.0, turned)).astype(BF16)
        ck[2 * g + 1] = (at_corner[at + TILE : at + 2 * TILE] + jnp.where(low8, 0.0, b)).astype(BF16)

    tile_here = pl.ds(pl.multiple_of(TILE * me, TILE), TILE)
    for k in FAR_FIRST:
        pltpu.make_async_remote_copy(
            hk.at[me ^ k], hb.at[tile_here, :], hsend, hrecv,
            device_id={"img": im, "depth": me ^ k}, device_id_type=MESH,
        ).start()
    pltpu.make_async_copy(hk.at[me], hb.at[tile_here, :], hrecv).start()

    @pl.when(has_left)
    def _():
        pl.semaphore_wait(go, 1)
        for k in range(ND):
            pltpu.make_async_remote_copy(
                ck.at[me ^ k], cb.at[tile_here, :], csend, crecv,
                device_id={"img": left, "depth": me ^ k}, device_id_type=MESH,
            ).start()

    send_chunk(2)
    pack(0)
    send_chunk(1)
    send_chunk(0)

    for c in range(NC + 1):
        rb[c, ND * CHUNK : (ND + 1) * CHUNK, :] = jnp.zeros((CHUNK, LANES), BF16)

    @pl.when(jnp.logical_not(has_right))
    def _():
        cb[...] = jnp.zeros((ND * TILE, LANES), BF16)

    code = jnp.floor(jnp.sqrt(table[...]) * (1.0 / UNIT) + 0.5)
    code = jnp.concatenate([code, code], 0).astype(I32)
    lane128 = iota((8, LANES), 1)
    even_of = (2 * lane128) & (LANES - 1)

    def every_other(offset):
        lo, hi = (
            jnp.take_along_axis(part, even_of + offset, axis=1, mode="promise_in_bounds")
            for part in (code[:, :LANES], code[:, LANES:])
        )
        return jnp.where(lane128 < LANES // 2, lo, hi)

    even_code, odd_code = every_other(0), every_other(1)
    next_code = jnp.where(lane128 == LANES - 1, odd_code, pltpu.roll(even_code, LANES - 1, 1))
    for c in range(4):
        words[c] = jnp.broadcast_to((even_code | (odd_code << 16))[c : c + 1], (8, LANES))
    for p in range(2):
        word = next_code[2 * p : 2 * p + 1] | (next_code[2 * p + 1 : 2 * p + 2] << 16)
        words[4 + p] = jnp.broadcast_to(word, (8, LANES))

    band[...] = band_matrix()

    load_entry.wait()
    low32 = iota((XH, LANES), 1) < YB
    even, odd = halves(ebuf[0:XH, :], ebuf[XH:XB, :], low32)
    ent[...] = jnp.where(lax.rem(me, 2) == 0, even, odd)

    is_edge = (iota((8, LANES), 1) & (YB - 1)) == YB - 1
    zero = jnp.zeros((8, LANES), F32)
    one = jnp.ones((8, LANES), F32)

    def make_edges(tiles):
        x = iota((XB, LANES), 0)
        dx = iota((XB, LANES), 1) - x
        sums = nt_dot(choose((dx >= 0) & (dx <= 1), SCALE), tiles)
        lane = iota((XB, LANES), 1)
        after = jnp.where(
            lane % TILE == ZB - 1,
            jnp.where(lane >= LANES - TILE, 0.0, pltpu.roll(sums, LANES - TILE + ZB - 1, 1)),
            pltpu.roll(sums, LANES - 1, 1),
        )
        sums += after
        front, back = halves(sums[:XH], sums[XH:], low32)
        return front, back

    def place_edges(t, front, back):
        for plane in range(NZ):
            d, r = plane // ZB, plane % ZB
            at = (YB - 1 - TILE * (d % 8) - r) % LANES
            edges[t, plane] = pltpu.roll((front, back)[d // 8][XT * t : XT * (t + 1)], at, 1)

    def lookup(scaled):
        lower = jnp.floor(scaled)
        frac = scaled - lower
        index = lower.astype(I32)
        odd = (index & 1) == 1
        within = lax.shift_right_logical(index, jnp.full_like(index, 1))

        def get(i):
            return jnp.take_along_axis(words[i], within, axis=1, mode="promise_in_bounds")

        values = []
        beyond = (get(4), get(5))
        for c in range(4):
            word = get(c)
            a = word & 65535
            b = lax.shift_right_logical(word, jnp.full_like(word, 16))
            e = beyond[c // 2]
            e = lax.shift_right_logical(e, jnp.full_like(e, 16)) if c % 2 else e & 65535
            lo = jnp.where(odd, b, a).astype(F32)
            hi = jnp.where(odd, e, b).astype(F32)
            lo = lo * lo
            hi = hi * hi
            values.append(lo + frac * (hi - lo))
        return values

    def wait_chunk(c):
        here = rb.at[c, pl.ds(0, ND * CHUNK), :]
        pltpu.make_async_copy(here, here, brecv.at[c]).wait()

    def column_tile(o, _):
        t = jnp.where(o == 0, 2, jnp.where(o == 1, 3, 3 - o))

        @pl.when(o == 0)
        def _():
            pltpu.make_async_copy(hb, hb, hrecv).wait()
            both = make_edges(hb[...])
            for t in range(NC - 1):
                place_edges(t, *both)
            wait_chunk(3)
            wait_chunk(2)

        @pl.when(o == 1)
        def _():
            @pl.when(has_right)
            def _():
                pltpu.make_async_copy(cb, cb, crecv).wait()

            hcb[...] = (hb[...].astype(F32) + cb[...].astype(F32)).astype(BF16)
            place_edges(NC - 1, *make_edges(hcb[...]))
            n = ND // 2
            row = iota((n * CHUNK, n * TILE), 0)
            src = iota((n * CHUNK, n * TILE), 1)
            grow = choose((row // CHUNK == src // TILE) & (row % XT == 0) & (src % TILE == ZB + row // XT % ZB))
            for p in range(2):
                rows = nn_dot(grow, hcb[p * n * TILE : (p + 1) * n * TILE, :])
                rb[NC, p * n * CHUNK : (p + 1) * n * CHUNK, :] = rows.astype(BF16)

        @pl.when(o == 2)
        def _():
            wait_chunk(1)

        @pl.when(o == 3)
        def _():
            wait_chunk(0)

        cols = pl.ds(pl.multiple_of(XT * t, XT), XT)
        for g in range(NZ // GROUP):
            at = GROUP * XT * g
            data = jnp.concatenate([rb[t, at : at + DEPTH, :], rb[t + 1, at : at + DEPTH, :]], 0)
            s = nn_dot(band[...], data)
            for z in range(GROUP):
                plane = GROUP * g + z
                value = s[XT * z : XT * (z + 1)]
                sbuf[plane] = value + jnp.where(is_edge, edges[t, plane], pltpu.roll(value, LANES - 1, 1))

        entry_here = ent[cols, :]

        def planes(i, carry):
            cum, bright, acc = carry
            acc = list(acc)
            for p in range(PLANES):
                plane = PLANES * i + p
                colour = lookup(sbuf[plane])
                cum = cum + jnp.where(entry_here <= plane, colour[3], 0.0)
                bright_next = jnp.exp2(cum * OPTICAL)
                weight = bright - bright_next
                bright = bright_next
                for c in range(3):
                    acc[c] = acc[c] + weight * colour[c]
            return cum, bright, tuple(acc)

        _, bright, acc = lax.fori_loop(0, NZ // PLANES, planes, (zero, one, (zero,) * 3))
        for c in range(3):
            result[c, cols, :] = acc[c] * (UNIT * UNIT)
        result[3, cols, :] = bright
        return 0

    lax.fori_loop(0, NC, column_tile, 0)
    turned = result[...].reshape(4 * XH, LANES).T
    for c in range(4):
        for h in range(2):
            out[c, :, XH * h : XH * (h + 1)] = turned[YB * h : YB * (h + 1), XH * c : XH * (c + 1)]

    sent = pk.at[pl.ds(0, NC * (ND - 1))]
    pltpu.make_async_copy(sent, sent, bsend).wait()
    tiles = hk.at[pl.ds(0, ND - 1)]
    pltpu.make_async_copy(tiles, tiles, hsend).wait()

    @pl.when(has_left)
    def _():
        pltpu.make_async_copy(ck, ck, csend).wait()


def shards(volume, entry_depth, tf_table):
    dma = pltpu.SemaphoreType.DMA
    return pl.pallas_call(
        kernel,
        out_shape=jax.ShapeDtypeStruct((4, YB, XB), F32),
        in_specs=[
            pl.BlockSpec(memory_space=pl.ANY),
            pl.BlockSpec(memory_space=pl.ANY),
            pl.BlockSpec(memory_space=pltpu.VMEM),
        ],
        out_specs=pl.BlockSpec(memory_space=pltpu.VMEM),
        scratch_shapes=[
            pltpu.VMEM((ZB, XB, NY), BF16),
            pltpu.VMEM((XB, LANES), I32),
            pltpu.VMEM((NC * ND, CHUNK, LANES), BF16),
            pltpu.VMEM((ND, TILE, LANES), BF16),
            pltpu.VMEM((ND, TILE, LANES), BF16),
            pltpu.VMEM((NC + 1, (ND + 1) * CHUNK, LANES), BF16),
            pltpu.VMEM((ND * TILE, LANES), BF16),
            pltpu.VMEM((ND * TILE, LANES), BF16),
            pltpu.VMEM((ND * TILE, LANES), BF16),
            pltpu.VMEM((6, 8, LANES), I32),
            pltpu.VMEM((XH, LANES), I32),
            pltpu.VMEM((GROUP * XT, 2 * DEPTH), BF16),
            pltpu.VMEM((NC, NZ, XT, LANES), F32),
            pltpu.VMEM((NZ, XT, LANES), F32),
            pltpu.VMEM((4, XH, LANES), F32),
            dma((4,)), dma, dma, dma, dma,
            dma((NC,)), dma, dma, pltpu.SemaphoreType.REGULAR,
        ],
        compiler_params=pltpu.CompilerParams(collective_id=0, has_side_effects=True),
        name="render",
    )(volume, entry_depth, tf_table.T)


def solution(mesh):
    placed = (P("depth", "img", None), P("img", None), P())
    return jax.shard_map(
        shards, mesh=mesh, in_specs=placed, out_specs=P(None, "depth", "img"), check_vma=False
    )
```

```python
import math

import jax
import jax.numpy as jnp
from jax import lax
from jax.experimental import pallas as pl
from jax.experimental.pallas import tpu as pltpu
from jax.sharding import PartitionSpec as P

MESH = pl.DeviceIdType.MESH
F32, BF16, I32 = jnp.float32, jnp.bfloat16, jnp.int32
ND = 16
NI = 16
ZB = 4
NZ = ND * ZB
XB = 64
XH = 32
XT = 8
NC = XH // XT
YB = 64
NY = ND * YB
LANES = 128
TILE = 8
CHUNK = ZB * XT
GROUP = 8
DEPTH = GROUP * XT + 2 * XT
SCALE = 255.0 / 16.0
UNIT = 2.0 / 65535.0
OPTICAL = -2.0 / NZ * math.log2(math.e) * UNIT * UNIT
PLANES = 64
FAR_FIRST = sorted(range(1, ND), key=lambda k: -((0, 1, 2, 1)[k & 3] + (0, 1, 2, 1)[k >> 2]))


def iota(shape, axis):
    return lax.broadcasted_iota(I32, shape, axis)


def choose(mask, value=1.0):
    return jnp.where(mask, value, 0.0).astype(BF16)


def nt_dot(a, b):
    return lax.dot_general(a, b, (((1,), (1,)), ((), ())), preferred_element_type=F32)


def nn_dot(a, b):
    return jnp.dot(a, b, preferred_element_type=F32)


def halves(a, b, low):
    turned = pltpu.roll(jnp.where(low, b, a), YB, 1)
    return jnp.where(low, a, turned), jnp.where(low, turned, b)


def band_matrix():
    row = iota((GROUP * XT, 2 * DEPTH), 0)
    col = iota((GROUP * XT, 2 * DEPTH), 1)
    second = col >= DEPTH
    local = jnp.where(second, col - DEPTH, col)
    dz = local // XT - row // XT
    dx = jnp.where(second, XT, 0) + local % XT - row % XT
    return choose((dz >= 0) & (dz <= 1) & (dx >= 0) & (dx <= 1), SCALE)


def kernel(
    vol, entry, table, out,
    vbuf, ebuf, pk, hk, ck, rb, hb, cb, hcb, words, ent, band, edges, sbuf, result,
    vsem, esem, bsend, hsend, csend, brecv, hrecv, crecv, go,
):
    me = lax.axis_index("depth")
    im = lax.axis_index("img")
    left = jnp.maximum(im - 1, 0)
    right = jnp.minimum(im + 1, NI - 1)
    has_left, has_right = im > 0, im < NI - 1

    def load(part, first):
        rows = pl.ds(first, 2 * XT)
        return pltpu.make_async_copy(vol.at[:, rows, :], vbuf.at[:, rows, :], vsem.at[part])

    firsts = (2 * XT, XH + 2 * XT, 0, XH)
    for part, first in enumerate(firsts):
        load(part, first).start()
    group = pl.multiple_of((me // 2) * LANES, LANES)
    load_entry = pltpu.make_async_copy(entry.at[:, pl.ds(group, LANES)], ebuf, esem)
    load_entry.start()

    barrier = pltpu.get_barrier_semaphore()
    for k in FAR_FIRST:
        pl.semaphore_signal(barrier, 1, device_id={"img": im, "depth": me ^ k}, device_id_type=MESH)

    @pl.when(has_left)
    def _():
        pl.semaphore_signal(barrier, 1, device_id={"img": left, "depth": me}, device_id_type=MESH)

    low = iota((2 * XT, LANES), 1) < YB
    low8 = iota((TILE, LANES), 1) < YB

    def pack(first_chunk):
        x = XT * first_chunk
        for g in range(ND // 2):
            lanes = slice(LANES * g, LANES * (g + 1))
            for z in range(ZB):
                pair = halves(vbuf[z, x : x + 2 * XT, lanes], vbuf[z, XH + x : XH + x + 2 * XT, lanes], low)
                for odd, v in enumerate(pair):
                    for c in range(2):
                        pk[(first_chunk + c) * ND + 2 * g + odd, XT * z : XT * (z + 1), :] = v[XT * c : XT * (c + 1)]

    def send_chunk(c):
        here = pl.ds(pl.multiple_of(CHUNK * me, CHUNK), CHUNK)
        for k in FAR_FIRST:
            pltpu.make_async_remote_copy(
                pk.at[c * ND + (me ^ k)], rb.at[c, here, :], bsend, brecv.at[c],
                device_id={"img": im, "depth": me ^ k}, device_id_type=MESH,
            ).start()
        pltpu.make_async_copy(pk.at[c * ND + me], rb.at[c, here, :], brecv.at[c]).start()

    load(0, firsts[0]).wait()
    load(1, firsts[1]).wait()
    pack(2)
    load(2, firsts[2]).wait()
    load(3, firsts[3]).wait()
    pack(0)
    sel = choose(iota((ND, NY), 1) == iota((ND, NY), 0) * YB + YB)
    zero_row = jnp.zeros((1, NY), F32)
    pad = jnp.zeros((ND, LANES - XB), F32)
    by_row = [jnp.concatenate([nt_dot(sel, vbuf[z]), pad], 1) for z in range(ZB)]
    first = jnp.concatenate([vbuf[z, 0:1, :].astype(F32) for z in range(ZB)] + [zero_row] * 4, 0)
    corner = nt_dot(sel, first.astype(BF16)).astype(BF16)
    spot = iota((LANES, ZB * ND), 0)
    block = iota((LANES, ZB * ND), 1)
    place = choose((spot // TILE == block % ND) & (spot % TILE == block // ND))
    mine = nn_dot(place, jnp.concatenate(by_row, 0).astype(BF16))
    spot16 = iota((LANES, ND), 0)
    spread = nn_dot(choose(spot16 // TILE == iota((LANES, ND), 1)), corner)
    lane8 = iota((LANES, TILE), 1)
    spread = jnp.sum(jnp.where(lane8 == iota((LANES, TILE), 0) % TILE, spread, 0.0), 1, keepdims=True)
    lane = iota((LANES, LANES), 1)
    at_corner = jnp.where((lane == YB) & (iota((LANES, LANES), 0) % TILE < ZB), jnp.broadcast_to(spread, (LANES, LANES)), 0.0)
    middle = jnp.concatenate([zero_row] * 4 + [vbuf[z, XH : XH + 1, :].astype(F32) for z in range(ZB)], 0)
    first = jnp.concatenate([zero_row] * 4 + [vbuf[z, 0:1, :].astype(F32) for z in range(ZB)], 0)
    for g in range(ND // 2):
        lanes = slice(LANES * g, LANES * (g + 1))
        a, b = middle[:, lanes], first[:, lanes]
        turned = pltpu.roll(jnp.where(low8, b, a), YB, 1)
        at = 2 * TILE * g
        hk[2 * g] = (mine[at : at + TILE] + jnp.where(low8, a, 0.0)).astype(BF16)
        hk[2 * g + 1] = (mine[at + TILE : at + 2 * TILE] + jnp.where(low8, turned, 0.0)).astype(BF16)
        ck[2 * g] = (at_corner[at : at + TILE] + jnp.where(low8, 0.0, turned)).astype(BF16)
        ck[2 * g + 1] = (at_corner[at + TILE : at + 2 * TILE] + jnp.where(low8, 0.0, b)).astype(BF16)

    pl.semaphore_wait(barrier, jnp.where(has_right, ND, ND - 1))

    @pl.when(has_right)
    def _():
        pl.semaphore_signal(go, 1, device_id={"img": right, "depth": me}, device_id_type=MESH)

    tile_here = pl.ds(pl.multiple_of(TILE * me, TILE), TILE)
    for k in FAR_FIRST:
        pltpu.make_async_remote_copy(
            hk.at[me ^ k], hb.at[tile_here, :], hsend, hrecv,
            device_id={"img": im, "depth": me ^ k}, device_id_type=MESH,
        ).start()
    pltpu.make_async_copy(hk.at[me], hb.at[tile_here, :], hrecv).start()

    send_chunk(3)
    send_chunk(2)

    @pl.when(has_left)
    def _():
        pl.semaphore_wait(go, 1)
        for k in range(ND):
            pltpu.make_async_remote_copy(
                ck.at[me ^ k], cb.at[tile_here, :], csend, crecv,
                device_id={"img": left, "depth": me ^ k}, device_id_type=MESH,
            ).start()

    send_chunk(1)
    send_chunk(0)

    for c in range(NC + 1):
        rb[c, ND * CHUNK : (ND + 1) * CHUNK, :] = jnp.zeros((CHUNK, LANES), BF16)

    @pl.when(jnp.logical_not(has_right))
    def _():
        cb[...] = jnp.zeros((ND * TILE, LANES), BF16)

    code = jnp.floor(jnp.sqrt(table[...]) * (1.0 / UNIT) + 0.5)
    code = jnp.concatenate([code, code], 0).astype(I32)
    lane128 = iota((8, LANES), 1)
    even_of = (2 * lane128) & (LANES - 1)

    def every_other(offset):
        lo, hi = (
            jnp.take_along_axis(part, even_of + offset, axis=1, mode="promise_in_bounds")
            for part in (code[:, :LANES], code[:, LANES:])
        )
        return jnp.where(lane128 < LANES // 2, lo, hi)

    even_code, odd_code = every_other(0), every_other(1)
    next_code = jnp.where(lane128 == LANES - 1, odd_code, pltpu.roll(even_code, LANES - 1, 1))
    for c in range(4):
        word = (odd_code | (even_code << 16)) if c % 2 else (even_code | (odd_code << 16))
        words[c] = jnp.broadcast_to(word[c : c + 1], (8, LANES))
    for p in range(2):
        word = next_code[2 * p : 2 * p + 1] | (next_code[2 * p + 1 : 2 * p + 2] << 16)
        words[4 + p] = jnp.broadcast_to(word, (8, LANES))

    band[...] = band_matrix()

    load_entry.wait()
    low32 = iota((XH, LANES), 1) < YB
    even, odd = halves(ebuf[0:XH, :], ebuf[XH:XB, :], low32)
    ent[...] = jnp.where(lax.rem(me, 2) == 0, even, odd)

    is_edge = (iota((8, LANES), 1) & (YB - 1)) == YB - 1
    zero = jnp.zeros((8, LANES), F32)
    one = jnp.ones((8, LANES), F32)

    def make_edges(tiles):
        x = iota((XB, LANES), 0)
        dx = iota((XB, LANES), 1) - x
        sums = nt_dot(choose((dx >= 0) & (dx <= 1), SCALE), tiles)
        lane = iota((XB, LANES), 1)
        after = jnp.where(
            lane % TILE == ZB - 1,
            jnp.where(lane >= LANES - TILE, 0.0, pltpu.roll(sums, LANES - TILE + ZB - 1, 1)),
            pltpu.roll(sums, LANES - 1, 1),
        )
        sums += after
        front, back = halves(sums[:XH], sums[XH:], low32)
        return front, back

    def place_edges(t, front, back):
        for plane in range(NZ):
            d, r = plane // ZB, plane % ZB
            at = (YB - 1 - TILE * (d % 8) - r) % LANES
            edges[t, plane] = pltpu.roll((front, back)[d // 8][XT * t : XT * (t + 1)], at, 1)

    def lookup(pairs):
        pair = pairs.astype(I32)
        r = pairs - pair.astype(F32)
        beyond = r >= 0.5
        away = jnp.abs(r + r - 1.0)

        def get(i):
            return jnp.take_along_axis(words[i], pair, axis=1, mode="promise_in_bounds")

        def upper(v):
            return lax.shift_right_logical(v, jnp.full_like(v, 16))

        def lower(v):
            return v & 65535

        values = []
        after = (get(4), get(5))
        for c in range(4):
            word = get(c)
            x = jnp.where(beyond, after[c // 2], word)
            x, b = (upper(x), lower(word)) if c % 2 else (lower(x), upper(word))
            x, b = x.astype(F32), b.astype(F32)
            x = x * x
            b = b * b
            values.append(b + away * (x - b))
        return values

    def wait_chunk(c):
        here = rb.at[c, pl.ds(0, ND * CHUNK), :]
        pltpu.make_async_copy(here, here, brecv.at[c]).wait()

    def column_tile(o, _):
        t = jnp.where(o == 0, 2, jnp.where(o == 1, 3, 3 - o))

        @pl.when(o == 0)
        def _():
            pltpu.make_async_copy(hb, hb, hrecv).wait()
            both = make_edges(hb[...])
            for t in range(NC - 1):
                place_edges(t, *both)
            wait_chunk(3)
            wait_chunk(2)

        @pl.when(o == 1)
        def _():
            @pl.when(has_right)
            def _():
                pltpu.make_async_copy(cb, cb, crecv).wait()

            hcb[...] = (hb[...].astype(F32) + cb[...].astype(F32)).astype(BF16)
            place_edges(NC - 1, *make_edges(hcb[...]))
            n = ND // 2
            row = iota((n * CHUNK, n * TILE), 0)
            src = iota((n * CHUNK, n * TILE), 1)
            grow = choose((row // CHUNK == src // TILE) & (row % XT == 0) & (src % TILE == ZB + row // XT % ZB))
            for p in range(2):
                rows = nn_dot(grow, hcb[p * n * TILE : (p + 1) * n * TILE, :])
                rb[NC, p * n * CHUNK : (p + 1) * n * CHUNK, :] = rows.astype(BF16)

        @pl.when(o == 2)
        def _():
            wait_chunk(1)

        @pl.when(o == 3)
        def _():
            wait_chunk(0)

        cols = pl.ds(pl.multiple_of(XT * t, XT), XT)
        for g in range(NZ // GROUP):
            at = GROUP * XT * g
            data = jnp.concatenate([rb[t, at : at + DEPTH, :], rb[t + 1, at : at + DEPTH, :]], 0)
            s = nn_dot(band[...], data)
            for z in range(GROUP):
                plane = GROUP * g + z
                value = s[XT * z : XT * (z + 1)]
                sbuf[plane] = value + jnp.where(is_edge, edges[t, plane], pltpu.roll(value, LANES - 1, 1))

        entry_here = ent[cols, :]

        def planes(i, carry):
            cum, bright, acc = carry
            acc = list(acc)
            for p in range(PLANES):
                plane = PLANES * i + p
                colour = lookup(sbuf[plane])
                cum = cum + jnp.where(entry_here <= plane, colour[3], 0.0)
                bright_next = jnp.exp2(cum * OPTICAL)
                weight = bright - bright_next
                bright = bright_next
                for c in range(3):
                    acc[c] = acc[c] + weight * colour[c]
            return cum, bright, tuple(acc)

        _, bright, acc = lax.fori_loop(0, NZ // PLANES, planes, (zero, one, (zero,) * 3))
        for c in range(3):
            result[c, cols, :] = acc[c] * (UNIT * UNIT)
        result[3, cols, :] = bright
        return 0

    lax.fori_loop(0, NC, column_tile, 0)
    turned = result[...].reshape(4 * XH, LANES).T
    for c in range(4):
        for h in range(2):
            out[c, :, XH * h : XH * (h + 1)] = turned[YB * h : YB * (h + 1), XH * c : XH * (c + 1)]

    sent = pk.at[pl.ds(0, NC * (ND - 1))]
    pltpu.make_async_copy(sent, sent, bsend).wait()
    tiles = hk.at[pl.ds(0, ND - 1)]
    pltpu.make_async_copy(tiles, tiles, hsend).wait()

    @pl.when(has_left)
    def _():
        pltpu.make_async_copy(ck, ck, csend).wait()


def shards(volume, entry_depth, tf_table):
    dma = pltpu.SemaphoreType.DMA
    return pl.pallas_call(
        kernel,
        out_shape=jax.ShapeDtypeStruct((4, YB, XB), F32),
        in_specs=[
            pl.BlockSpec(memory_space=pl.ANY),
            pl.BlockSpec(memory_space=pl.ANY),
            pl.BlockSpec(memory_space=pltpu.VMEM),
        ],
        out_specs=pl.BlockSpec(memory_space=pltpu.VMEM),
        scratch_shapes=[
            pltpu.VMEM((ZB, XB, NY), BF16),
            pltpu.VMEM((XB, LANES), I32),
            pltpu.VMEM((NC * ND, CHUNK, LANES), BF16),
            pltpu.VMEM((ND, TILE, LANES), BF16),
            pltpu.VMEM((ND, TILE, LANES), BF16),
            pltpu.VMEM((NC + 1, (ND + 1) * CHUNK, LANES), BF16),
            pltpu.VMEM((ND * TILE, LANES), BF16),
            pltpu.VMEM((ND * TILE, LANES), BF16),
            pltpu.VMEM((ND * TILE, LANES), BF16),
            pltpu.VMEM((6, 8, LANES), I32),
            pltpu.VMEM((XH, LANES), I32),
            pltpu.VMEM((GROUP * XT, 2 * DEPTH), BF16),
            pltpu.VMEM((NC, NZ, XT, LANES), F32),
            pltpu.VMEM((NZ, XT, LANES), F32),
            pltpu.VMEM((4, XH, LANES), F32),
            dma((4,)), dma, dma, dma, dma,
            dma((NC,)), dma, dma, pltpu.SemaphoreType.REGULAR,
        ],
        compiler_params=pltpu.CompilerParams(collective_id=0, has_side_effects=True),
        name="render",
    )(volume, entry_depth, tf_table.T)


def solution(mesh):
    placed = (P("depth", "img", None), P("img", None), P())
    return jax.shard_map(
        shards, mesh=mesh, in_specs=placed, out_specs=P(None, "depth", "img"), check_vma=False
    )
```

```python
import math

import jax
import jax.numpy as jnp
from jax import lax
from jax.experimental import pallas as pl
from jax.experimental.pallas import tpu as pltpu
from jax.sharding import PartitionSpec as P

MESH = pl.DeviceIdType.MESH
F32, BF16, I32 = jnp.float32, jnp.bfloat16, jnp.int32
ND = 16
NI = 16
ZB = 4
NZ = ND * ZB
XB = 64
XH = 32
XT = 8
NC = XH // XT
YB = 64
NY = ND * YB
LANES = 128
TILE = 8
CHUNK = ZB * XT
GROUP = 8
DEPTH = GROUP * XT + 2 * XT
SIDE = 4 * TILE
SCALE = 255.0 / 16.0
UNIT = 2.0 / 65535.0
OPTICAL = -2.0 / NZ * math.log2(math.e) * UNIT * UNIT
PLANES = 64
FAR_FIRST = sorted(range(1, ND), key=lambda k: -((0, 1, 2, 1)[k & 3] + (0, 1, 2, 1)[k >> 2]))


def iota(shape, axis):
    return lax.broadcasted_iota(I32, shape, axis)


def choose(mask, value=1.0):
    return jnp.where(mask, value, 0.0).astype(BF16)


def nt_dot(a, b):
    return lax.dot_general(a, b, (((1,), (1,)), ((), ())), preferred_element_type=F32)


def nn_dot(a, b):
    return jnp.dot(a, b, preferred_element_type=F32)


def halves(a, b, low):
    turned = pltpu.roll(jnp.where(low, b, a), YB, 1)
    return jnp.where(low, a, turned), jnp.where(low, turned, b)


def band_matrix():
    row = iota((GROUP * XT, 2 * DEPTH), 0)
    col = iota((GROUP * XT, 2 * DEPTH), 1)
    second = col >= DEPTH
    local = jnp.where(second, col - DEPTH, col)
    dz = local // XT - row // XT
    dx = jnp.where(second, XT, 0) + local % XT - row % XT
    return choose((dz >= 0) & (dz <= 1) & (dx >= 0) & (dx <= 1), SCALE)


def side_matrix():
    row = iota((GROUP * XT, DEPTH + SIDE), 0)
    col = iota((GROUP * XT, DEPTH + SIDE), 1)
    tile = col - DEPTH
    second = tile >= 0
    dz = jnp.where(second, tile // TILE * ZB + tile % TILE - ZB, col // XT) - row // XT
    dx = jnp.where(second, XT, col % XT) - row % XT
    used = (tile < 0) | (tile % TILE >= ZB)
    return choose(used & (dz >= 0) & (dz <= 1) & (dx >= 0) & (dx <= 1), SCALE)


def kernel(
    vol, entry, table, out,
    vbuf, ebuf, tbuf, pk, hk, ck, rb, hb, cb, hcb, words, ent, band, side_band, pair, edges, sbuf, result,
    vsem, esem, tsem, bsend, hsend, csend, brecv, hrecv, crecv, go,
):
    me = lax.axis_index("depth")
    im = lax.axis_index("img")
    left = jnp.maximum(im - 1, 0)
    right = jnp.minimum(im + 1, NI - 1)
    has_left, has_right = im > 0, im < NI - 1

    def load(part, first):
        rows = pl.ds(first, 2 * XT)
        return pltpu.make_async_copy(vol.at[:, rows, :], vbuf.at[:, rows, :], vsem.at[part])

    firsts = (2 * XT, XH + 2 * XT, 0, XH)
    for part, first in enumerate(firsts):
        load(part, first).start()
    group = pl.multiple_of((me // 2) * LANES, LANES)
    load_entry = pltpu.make_async_copy(entry.at[:, pl.ds(group, LANES)], ebuf, esem)
    load_entry.start()
    load_table = pltpu.make_async_copy(table, tbuf, tsem)
    load_table.start()

    barrier = pltpu.get_barrier_semaphore()
    for k in FAR_FIRST:
        pl.semaphore_signal(barrier, 1, device_id={"img": im, "depth": me ^ k}, device_id_type=MESH)

    @pl.when(has_left)
    def _():
        pl.semaphore_signal(barrier, 1, device_id={"img": left, "depth": me}, device_id_type=MESH)

    low = iota((2 * XT, LANES), 1) < YB
    low8 = iota((TILE, LANES), 1) < YB

    def pack(first_chunk):
        x = XT * first_chunk
        for g in range(ND // 2):
            lanes = slice(LANES * g, LANES * (g + 1))
            for z in range(ZB):
                pair = halves(vbuf[z, x : x + 2 * XT, lanes], vbuf[z, XH + x : XH + x + 2 * XT, lanes], low)
                for odd, v in enumerate(pair):
                    for c in range(2):
                        pk[(first_chunk + c) * ND + 2 * g + odd, XT * z : XT * (z + 1), :] = v[XT * c : XT * (c + 1)]

    def send_chunk(c):
        here = pl.ds(pl.multiple_of(CHUNK * me, CHUNK), CHUNK)
        for k in FAR_FIRST:
            pltpu.make_async_remote_copy(
                pk.at[c * ND + (me ^ k)], rb.at[c, here, :], bsend, brecv.at[c],
                device_id={"img": im, "depth": me ^ k}, device_id_type=MESH,
            ).start()
        pltpu.make_async_copy(pk.at[c * ND + me], rb.at[c, here, :], brecv.at[c]).start()

    load(0, firsts[0]).wait()
    load(1, firsts[1]).wait()
    pack(2)
    load(2, firsts[2]).wait()
    load(3, firsts[3]).wait()
    pack(0)
    sel = choose(iota((ND, NY), 1) == iota((ND, NY), 0) * YB + YB)
    zero_row = jnp.zeros((1, NY), F32)
    pad = jnp.zeros((ND, LANES - XB), F32)
    by_row = [jnp.concatenate([nt_dot(sel, vbuf[z]), pad], 1) for z in range(ZB)]
    first = jnp.concatenate([vbuf[z, 0:1, :].astype(F32) for z in range(ZB)] + [zero_row] * 4, 0)
    corner = nt_dot(sel, first.astype(BF16)).astype(BF16)
    spot = iota((LANES, ZB * ND), 0)
    block = iota((LANES, ZB * ND), 1)
    place = choose((spot // TILE == block % ND) & (spot % TILE == block // ND))
    mine = nn_dot(place, jnp.concatenate(by_row, 0).astype(BF16))
    spot16 = iota((LANES, ND), 0)
    spread = nn_dot(choose(spot16 // TILE == iota((LANES, ND), 1)), corner)
    lane8 = iota((LANES, TILE), 1)
    spread = jnp.sum(jnp.where(lane8 == iota((LANES, TILE), 0) % TILE, spread, 0.0), 1, keepdims=True)
    lane = iota((LANES, LANES), 1)
    at_corner = jnp.where((lane == YB) & (iota((LANES, LANES), 0) % TILE < ZB), jnp.broadcast_to(spread, (LANES, LANES)), 0.0)
    middle = jnp.concatenate([zero_row] * 4 + [vbuf[z, XH : XH + 1, :].astype(F32) for z in range(ZB)], 0)
    first = jnp.concatenate([zero_row] * 4 + [vbuf[z, 0:1, :].astype(F32) for z in range(ZB)], 0)
    for g in range(ND // 2):
        lanes = slice(LANES * g, LANES * (g + 1))
        a, b = middle[:, lanes], first[:, lanes]
        turned = pltpu.roll(jnp.where(low8, b, a), YB, 1)
        at = 2 * TILE * g
        hk[2 * g] = (mine[at : at + TILE] + jnp.where(low8, a, 0.0)).astype(BF16)
        hk[2 * g + 1] = (mine[at + TILE : at + 2 * TILE] + jnp.where(low8, turned, 0.0)).astype(BF16)
        ck[2 * g] = (at_corner[at : at + TILE] + jnp.where(low8, 0.0, turned)).astype(BF16)
        ck[2 * g + 1] = (at_corner[at + TILE : at + 2 * TILE] + jnp.where(low8, 0.0, b)).astype(BF16)

    hcb[ND * TILE : (ND + 2) * TILE, :] = jnp.zeros((2 * TILE, LANES), BF16)
    for c in range(NC):
        rb[c, ND * CHUNK : (ND + 1) * CHUNK, :] = jnp.zeros((CHUNK, LANES), BF16)

    @pl.when(jnp.logical_not(has_right))
    def _():
        cb[...] = jnp.zeros((ND * TILE, LANES), BF16)

    load_table.wait()
    code = jnp.floor(jnp.sqrt(tbuf[...]) * (1.0 / UNIT) + 0.5)
    code = jnp.concatenate([code, code], 0).astype(I32)
    lane128 = iota((8, LANES), 1)
    even_of = (2 * lane128) & (LANES - 1)

    def every_other(offset):
        lo, hi = (
            jnp.take_along_axis(part, even_of + offset, axis=1, mode="promise_in_bounds")
            for part in (code[:, :LANES], code[:, LANES:])
        )
        return jnp.where(lane128 < LANES // 2, lo, hi)

    even_code, odd_code = every_other(0), every_other(1)
    next_code = jnp.where(lane128 == LANES - 1, odd_code, pltpu.roll(even_code, LANES - 1, 1))
    for c in range(4):
        word = (odd_code | (even_code << 16)) if c % 2 else (even_code | (odd_code << 16))
        words[c] = jnp.broadcast_to(word[c : c + 1], (8, LANES))
    for p in range(2):
        word = next_code[2 * p : 2 * p + 1] | (next_code[2 * p + 1 : 2 * p + 2] << 16)
        words[4 + p] = jnp.broadcast_to(word, (8, LANES))

    band[...] = band_matrix()
    side_band[...] = side_matrix()
    dx = iota((XB, LANES), 1) - iota((XB, LANES), 0)
    pair[...] = choose((dx >= 0) & (dx <= 1), SCALE)

    pl.semaphore_wait(barrier, jnp.where(has_right, ND, ND - 1))

    @pl.when(has_right)
    def _():
        pl.semaphore_signal(go, 1, device_id={"img": right, "depth": me}, device_id_type=MESH)

    tile_here = pl.ds(pl.multiple_of(TILE * me, TILE), TILE)
    for k in FAR_FIRST:
        pltpu.make_async_remote_copy(
            hk.at[me ^ k], hb.at[tile_here, :], hsend, hrecv,
            device_id={"img": im, "depth": me ^ k}, device_id_type=MESH,
        ).start()
    pltpu.make_async_copy(hk.at[me], hb.at[tile_here, :], hrecv).start()

    send_chunk(3)
    send_chunk(2)

    @pl.when(has_left)
    def _():
        pl.semaphore_wait(go, 1)
        for k in range(ND):
            pltpu.make_async_remote_copy(
                ck.at[me ^ k], cb.at[tile_here, :], csend, crecv,
                device_id={"img": left, "depth": me ^ k}, device_id_type=MESH,
            ).start()

    send_chunk(1)
    send_chunk(0)

    load_entry.wait()
    low32 = iota((XH, LANES), 1) < YB
    even, odd = halves(ebuf[0:XH, :], ebuf[XH:XB, :], low32)
    ent[...] = jnp.where(lax.rem(me, 2) == 0, even, odd)

    is_edge = (iota((8, LANES), 1) & (YB - 1)) == YB - 1
    zero = jnp.zeros((8, LANES), F32)
    one = jnp.ones((8, LANES), F32)

    def make_edges(left_rows, right_rows, tiles, is_low):
        n = left_rows.shape[0]
        sums = nt_dot(jnp.concatenate([left_rows, right_rows], 0), tiles)
        lane = iota((2 * n, LANES), 1)
        after = jnp.where(
            lane % TILE == ZB - 1,
            jnp.where(lane >= LANES - TILE, 0.0, pltpu.roll(sums, LANES - TILE + ZB - 1, 1)),
            pltpu.roll(sums, LANES - 1, 1),
        )
        sums += after
        return halves(sums[:n], sums[n:], is_low)

    def place_edges(t, front, back):
        for plane in range(NZ):
            d, r = plane // ZB, plane % ZB
            at = (YB - 1 - TILE * (d % 8) - r) % LANES
            edges[t, plane] = pltpu.roll((front, back)[d // 8], at, 1)

    def lookup(pairs):
        pair = pairs.astype(I32)
        r = pairs - pair.astype(F32)
        beyond = r >= 0.5
        away = jnp.abs(r + r - 1.0)

        def get(i):
            return jnp.take_along_axis(words[i], pair, axis=1, mode="promise_in_bounds")

        def upper(v):
            return lax.shift_right_logical(v, jnp.full_like(v, 16))

        def lower(v):
            return v & 65535

        values = []
        after = (get(4), get(5))
        for c in range(4):
            word = get(c)
            x = jnp.where(beyond, after[c // 2], word)
            x, b = (upper(x), lower(word)) if c % 2 else (lower(x), upper(word))
            x, b = x.astype(F32), b.astype(F32)
            x = x * x
            b = b * b
            values.append(b + away * (x - b))
        return values

    def wait_chunk(c):
        here = rb.at[c, pl.ds(0, ND * CHUNK), :]
        pltpu.make_async_copy(here, here, brecv.at[c]).wait()

    def store_sums(g, t, s):
        for z in range(GROUP):
            plane = GROUP * g + z
            value = s[XT * z : XT * (z + 1)]
            sbuf[plane] = value + jnp.where(is_edge, edges[t, plane], pltpu.roll(value, LANES - 1, 1))

    def column_tile(o, _):
        t = jnp.where(o == 0, 2, jnp.where(o == 1, 3, 3 - o))

        @pl.when(o == 0)
        def _():
            pltpu.make_async_copy(hb, hb, hrecv).wait()
            front, back = make_edges(pair[0:XH, :], pair[XH:XB, :], hb[...], low32)
            for t in range(NC - 1):
                place_edges(t, front[XT * t : XT * (t + 1)], back[XT * t : XT * (t + 1)])
            wait_chunk(3)
            wait_chunk(2)

        @pl.when(o == 1)
        def _():
            @pl.when(has_right)
            def _():
                pltpu.make_async_copy(cb, cb, crecv).wait()

            hcb[0 : ND * TILE, :] = (hb[...].astype(F32) + cb[...].astype(F32)).astype(BF16)
            place_edges(NC - 1, *make_edges(pair[XH - XT : XH, :], pair[XB - XT : XB, :], hcb[0 : ND * TILE, :], low8))
            for g in range(NZ // GROUP):
                at = GROUP * XT * g
                tiles = hcb[2 * TILE * g : 2 * TILE * g + SIDE, :]
                store_sums(g, NC - 1, nn_dot(side_band[...], jnp.concatenate([rb[NC - 1, at : at + DEPTH, :], tiles], 0)))

        @pl.when(o == 2)
        def _():
            wait_chunk(1)

        @pl.when(o == 3)
        def _():
            wait_chunk(0)

        cols = pl.ds(pl.multiple_of(XT * t, XT), XT)
        @pl.when(o != 1)
        def _():
            for g in range(NZ // GROUP):
                at = GROUP * XT * g
                data = jnp.concatenate([rb[t, at : at + DEPTH, :], rb[t + 1, at : at + DEPTH, :]], 0)
                store_sums(g, t, nn_dot(band[...], data))

        entry_here = ent[cols, :]

        def planes(i, carry):
            cum, bright, acc = carry
            acc = list(acc)
            for p in range(PLANES):
                plane = PLANES * i + p
                colour = lookup(sbuf[plane])
                cum = cum + jnp.where(entry_here <= plane, colour[3], 0.0)
                bright_next = jnp.exp2(cum * OPTICAL)
                weight = bright - bright_next
                bright = bright_next
                for c in range(3):
                    acc[c] = acc[c] + weight * colour[c]
            return cum, bright, tuple(acc)

        _, bright, acc = lax.fori_loop(0, NZ // PLANES, planes, (zero, one, (zero,) * 3))
        for c in range(3):
            result[c, cols, :] = acc[c] * (UNIT * UNIT)
        result[3, cols, :] = bright
        return 0

    lax.fori_loop(0, NC, column_tile, 0)
    turned = result[...].reshape(4 * XH, LANES).T
    for c in range(4):
        for h in range(2):
            out[c, :, XH * h : XH * (h + 1)] = turned[YB * h : YB * (h + 1), XH * c : XH * (c + 1)]

    sent = pk.at[pl.ds(0, NC * (ND - 1))]
    pltpu.make_async_copy(sent, sent, bsend).wait()
    tiles = hk.at[pl.ds(0, ND - 1)]
    pltpu.make_async_copy(tiles, tiles, hsend).wait()

    @pl.when(has_left)
    def _():
        pltpu.make_async_copy(ck, ck, csend).wait()


def shards(volume, entry_depth, tf_table):
    dma = pltpu.SemaphoreType.DMA
    return pl.pallas_call(
        kernel,
        out_shape=jax.ShapeDtypeStruct((4, YB, XB), F32),
        in_specs=[
            pl.BlockSpec(memory_space=pl.ANY),
            pl.BlockSpec(memory_space=pl.ANY),
            pl.BlockSpec(memory_space=pl.ANY),
        ],
        out_specs=pl.BlockSpec(memory_space=pltpu.VMEM),
        scratch_shapes=[
            pltpu.VMEM((ZB, XB, NY), BF16),
            pltpu.VMEM((XB, LANES), I32),
            pltpu.VMEM((4, 2 * LANES), F32),
            pltpu.VMEM((NC * ND, CHUNK, LANES), BF16),
            pltpu.VMEM((ND, TILE, LANES), BF16),
            pltpu.VMEM((ND, TILE, LANES), BF16),
            pltpu.VMEM((NC, (ND + 1) * CHUNK, LANES), BF16),
            pltpu.VMEM((ND * TILE, LANES), BF16),
            pltpu.VMEM((ND * TILE, LANES), BF16),
            pltpu.VMEM(((ND + 2) * TILE, LANES), BF16),
            pltpu.VMEM((6, 8, LANES), I32),
            pltpu.VMEM((XH, LANES), I32),
            pltpu.VMEM((GROUP * XT, 2 * DEPTH), BF16),
            pltpu.VMEM((GROUP * XT, DEPTH + SIDE), BF16),
            pltpu.VMEM((XB, LANES), BF16),
            pltpu.VMEM((NC, NZ, XT, LANES), F32),
            pltpu.VMEM((NZ, XT, LANES), F32),
            pltpu.VMEM((4, XH, LANES), F32),
            dma((4,)), dma, dma, dma, dma, dma,
            dma((NC,)), dma, dma, pltpu.SemaphoreType.REGULAR,
        ],
        compiler_params=pltpu.CompilerParams(collective_id=0, has_side_effects=True),
        name="render",
    )(volume, entry_depth, tf_table.T)


def solution(mesh):
    placed = (P("depth", "img", None), P("img", None), P())
    return jax.shard_map(
        shards, mesh=mesh, in_specs=placed, out_specs=P(None, "depth", "img"), check_vma=False
    )
```

```python
import math

import jax
import jax.numpy as jnp
from jax import lax
from jax.experimental import pallas as pl
from jax.experimental.pallas import tpu as pltpu
from jax.sharding import PartitionSpec as P

MESH = pl.DeviceIdType.MESH
F32, BF16, I32 = jnp.float32, jnp.bfloat16, jnp.int32
ND = 16
NI = 16
ZB = 4
NZ = ND * ZB
XB = 64
XH = 32
XT = 8
NC = XH // XT
YB = 64
NY = ND * YB
LANES = 128
TILE = 8
CHUNK = ZB * XT
GROUP = 8
DEPTH = GROUP * XT + 2 * XT
SIDE = 4 * TILE
SCALE = 255.0 / 16.0
UNIT = 2.0 / 65535.0
OPTICAL = -2.0 / NZ * math.log2(math.e) * UNIT * UNIT
PLANES = 64
FAR_FIRST = sorted(range(1, ND), key=lambda k: -((0, 1, 2, 1)[k & 3] + (0, 1, 2, 1)[k >> 2]))


def iota(shape, axis):
    return lax.broadcasted_iota(I32, shape, axis)


def choose(mask, value=1.0):
    return jnp.where(mask, value, 0.0).astype(BF16)


def nt_dot(a, b):
    return lax.dot_general(a, b, (((1,), (1,)), ((), ())), preferred_element_type=F32)


def nn_dot(a, b):
    return jnp.dot(a, b, preferred_element_type=F32)


def halves(a, b, low):
    turned = pltpu.roll(jnp.where(low, b, a), YB, 1)
    return jnp.where(low, a, turned), jnp.where(low, turned, b)


def band_matrix():
    row = iota((GROUP * XT, 2 * DEPTH), 0)
    col = iota((GROUP * XT, 2 * DEPTH), 1)
    second = col >= DEPTH
    local = jnp.where(second, col - DEPTH, col)
    dz = local // XT - row // XT
    dx = jnp.where(second, XT, 0) + local % XT - row % XT
    return choose((dz >= 0) & (dz <= 1) & (dx >= 0) & (dx <= 1), SCALE)


def side_matrix():
    row = iota((GROUP * XT, DEPTH + SIDE), 0)
    col = iota((GROUP * XT, DEPTH + SIDE), 1)
    tile = col - DEPTH
    second = tile >= 0
    dz = jnp.where(second, tile // TILE * ZB + tile % TILE - ZB, col // XT) - row // XT
    dx = jnp.where(second, XT, col % XT) - row % XT
    used = (tile < 0) | (tile % TILE >= ZB)
    return choose(used & (dz >= 0) & (dz <= 1) & (dx >= 0) & (dx <= 1), SCALE)


def kernel(
    vol, entry, table, result,
    vbuf, ebuf, tbuf, pk, hk, ck, rb, hb, cb, hcb, words, ent, band, side_band, pair, edges, sbuf,
    vsem, esem, tsem, bsend, hsend, csend, brecv, hrecv, crecv, go,
):
    me = lax.axis_index("depth")
    im = lax.axis_index("img")
    left = jnp.maximum(im - 1, 0)
    right = jnp.minimum(im + 1, NI - 1)
    has_left, has_right = im > 0, im < NI - 1

    def load(part, first):
        rows = pl.ds(first, 2 * XT)
        return pltpu.make_async_copy(vol.at[:, rows, :], vbuf.at[:, rows, :], vsem.at[part])

    firsts = (2 * XT, XH + 2 * XT, 0, XH)
    for part, first in enumerate(firsts):
        load(part, first).start()
    group = pl.multiple_of((me // 2) * LANES, LANES)
    load_entry = pltpu.make_async_copy(entry.at[:, pl.ds(group, LANES)], ebuf, esem)
    load_entry.start()
    load_table = pltpu.make_async_copy(table, tbuf, tsem)
    load_table.start()

    barrier = pltpu.get_barrier_semaphore()
    for k in FAR_FIRST:
        pl.semaphore_signal(barrier, 1, device_id={"img": im, "depth": me ^ k}, device_id_type=MESH)

    @pl.when(has_left)
    def _():
        pl.semaphore_signal(barrier, 1, device_id={"img": left, "depth": me}, device_id_type=MESH)

    low = iota((2 * XT, LANES), 1) < YB
    low8 = iota((TILE, LANES), 1) < YB

    def pack(first_chunk):
        x = XT * first_chunk
        for g in range(ND // 2):
            lanes = slice(LANES * g, LANES * (g + 1))
            for z in range(ZB):
                pair = halves(vbuf[z, x : x + 2 * XT, lanes], vbuf[z, XH + x : XH + x + 2 * XT, lanes], low)
                for odd, v in enumerate(pair):
                    for c in range(2):
                        pk[first_chunk + c, 2 * g + odd, XT * z : XT * (z + 1), :] = v[XT * c : XT * (c + 1)]

    def send_chunk(c, n=1):
        here = pl.ds(pl.multiple_of(CHUNK * me, CHUNK), CHUNK)
        for k in FAR_FIRST:
            pltpu.make_async_remote_copy(
                pk.at[pl.ds(c, n), me ^ k], rb.at[pl.ds(c, n), here, :], bsend, brecv.at[c],
                device_id={"img": im, "depth": me ^ k}, device_id_type=MESH,
            ).start()
        pltpu.make_async_copy(pk.at[pl.ds(c, n), me], rb.at[pl.ds(c, n), here, :], brecv.at[c]).start()

    load(0, firsts[0]).wait()
    load(1, firsts[1]).wait()
    pack(2)
    load(2, firsts[2]).wait()
    load(3, firsts[3]).wait()
    pack(0)
    sel = choose(iota((ND, NY), 1) == iota((ND, NY), 0) * YB + YB)
    zero_row = jnp.zeros((1, NY), F32)
    pad = jnp.zeros((ND, LANES - XB), F32)
    by_row = [jnp.concatenate([nt_dot(sel, vbuf[z]), pad], 1) for z in range(ZB)]
    first = jnp.concatenate([vbuf[z, 0:1, :].astype(F32) for z in range(ZB)] + [zero_row] * 4, 0)
    corner = nt_dot(sel, first.astype(BF16)).astype(BF16)
    spot = iota((LANES, ZB * ND), 0)
    block = iota((LANES, ZB * ND), 1)
    place = choose((spot // TILE == block % ND) & (spot % TILE == block // ND))
    mine = nn_dot(place, jnp.concatenate(by_row, 0).astype(BF16))
    spot16 = iota((LANES, ND), 0)
    spread = nn_dot(choose(spot16 // TILE == iota((LANES, ND), 1)), corner)
    lane8 = iota((LANES, TILE), 1)
    spread = jnp.sum(jnp.where(lane8 == iota((LANES, TILE), 0) % TILE, spread, 0.0), 1, keepdims=True)
    lane = iota((LANES, LANES), 1)
    at_corner = jnp.where((lane == YB) & (iota((LANES, LANES), 0) % TILE < ZB), jnp.broadcast_to(spread, (LANES, LANES)), 0.0)
    middle = jnp.concatenate([zero_row] * 4 + [vbuf[z, XH : XH + 1, :].astype(F32) for z in range(ZB)], 0)
    first = jnp.concatenate([zero_row] * 4 + [vbuf[z, 0:1, :].astype(F32) for z in range(ZB)], 0)
    for g in range(ND // 2):
        lanes = slice(LANES * g, LANES * (g + 1))
        a, b = middle[:, lanes], first[:, lanes]
        turned = pltpu.roll(jnp.where(low8, b, a), YB, 1)
        at = 2 * TILE * g
        hk[2 * g] = (mine[at : at + TILE] + jnp.where(low8, a, 0.0)).astype(BF16)
        hk[2 * g + 1] = (mine[at + TILE : at + 2 * TILE] + jnp.where(low8, turned, 0.0)).astype(BF16)
        ck[2 * g] = (at_corner[at : at + TILE] + jnp.where(low8, 0.0, turned)).astype(BF16)
        ck[2 * g + 1] = (at_corner[at + TILE : at + 2 * TILE] + jnp.where(low8, 0.0, b)).astype(BF16)

    hcb[ND * TILE : (ND + 2) * TILE, :] = jnp.zeros((2 * TILE, LANES), BF16)
    for c in range(NC):
        rb[c, ND * CHUNK : (ND + 1) * CHUNK, :] = jnp.zeros((CHUNK, LANES), BF16)

    @pl.when(jnp.logical_not(has_right))
    def _():
        cb[...] = jnp.zeros((ND * TILE, LANES), BF16)

    load_table.wait()
    code = jnp.floor(jnp.sqrt(tbuf[...]) * (1.0 / UNIT) + 0.5)
    code = jnp.concatenate([code, code], 0).astype(I32)
    lane128 = iota((8, LANES), 1)
    even_of = (2 * lane128) & (LANES - 1)

    def every_other(offset):
        lo, hi = (
            jnp.take_along_axis(part, even_of + offset, axis=1, mode="promise_in_bounds")
            for part in (code[:, :LANES], code[:, LANES:])
        )
        return jnp.where(lane128 < LANES // 2, lo, hi)

    even_code, odd_code = every_other(0), every_other(1)
    next_code = jnp.where(lane128 == LANES - 1, odd_code, pltpu.roll(even_code, LANES - 1, 1))
    for c in range(4):
        word = (odd_code | (even_code << 16)) if c % 2 else (even_code | (odd_code << 16))
        words[c] = jnp.broadcast_to(word[c : c + 1], (8, LANES))
    for p in range(2):
        word = next_code[2 * p : 2 * p + 1] | (next_code[2 * p + 1 : 2 * p + 2] << 16)
        words[4 + p] = jnp.broadcast_to(word, (8, LANES))

    band[...] = band_matrix()
    side_band[...] = side_matrix()
    dx = iota((XB, LANES), 1) - iota((XB, LANES), 0)
    pair[...] = choose((dx >= 0) & (dx <= 1), SCALE)

    pl.semaphore_wait(barrier, jnp.where(has_right, ND, ND - 1))

    @pl.when(has_right)
    def _():
        pl.semaphore_signal(go, 1, device_id={"img": right, "depth": me}, device_id_type=MESH)

    tile_here = pl.ds(pl.multiple_of(TILE * me, TILE), TILE)
    for k in FAR_FIRST:
        pltpu.make_async_remote_copy(
            hk.at[me ^ k], hb.at[tile_here, :], hsend, hrecv,
            device_id={"img": im, "depth": me ^ k}, device_id_type=MESH,
        ).start()
    pltpu.make_async_copy(hk.at[me], hb.at[tile_here, :], hrecv).start()

    send_chunk(2, 2)

    @pl.when(has_left)
    def _():
        pl.semaphore_wait(go, 1)
        for k in FAR_FIRST + [0]:
            pltpu.make_async_remote_copy(
                ck.at[me ^ k], cb.at[tile_here, :], csend, crecv,
                device_id={"img": left, "depth": me ^ k}, device_id_type=MESH,
            ).start()

    send_chunk(1)
    send_chunk(0)

    load_entry.wait()
    low32 = iota((XH, LANES), 1) < YB
    even, odd = halves(ebuf[0:XH, :], ebuf[XH:XB, :], low32)
    ent[...] = jnp.where(lax.rem(me, 2) == 0, even, odd)

    is_edge = (iota((8, LANES), 1) & (YB - 1)) == YB - 1
    zero = jnp.zeros((8, LANES), F32)
    one = jnp.ones((8, LANES), F32)

    def make_edges(left_rows, right_rows, tiles, is_low):
        n = left_rows.shape[0]
        sums = nt_dot(jnp.concatenate([left_rows, right_rows], 0), tiles)
        lane = iota((2 * n, LANES), 1)
        after = jnp.where(
            lane % TILE == ZB - 1,
            jnp.where(lane >= LANES - TILE, 0.0, pltpu.roll(sums, LANES - TILE + ZB - 1, 1)),
            pltpu.roll(sums, LANES - 1, 1),
        )
        sums += after
        return halves(sums[:n], sums[n:], is_low)

    def place_edges(t, front, back):
        for plane in range(NZ):
            d, r = plane // ZB, plane % ZB
            at = (YB - 1 - TILE * (d % 8) - r) % LANES
            edges[t, plane] = pltpu.roll((front, back)[d // 8], at, 1)

    def lookup(pairs):
        pair = pairs.astype(I32)
        r = pairs - pair.astype(F32)
        beyond = r >= 0.5
        away = jnp.abs(r + r - 1.0)

        def get(i):
            return jnp.take_along_axis(words[i], pair, axis=1, mode="promise_in_bounds")

        def upper(v):
            return lax.shift_right_logical(v, jnp.full_like(v, 16))

        def lower(v):
            return v & 65535

        values = []
        after = (get(4), get(5))
        for c in range(4):
            word = get(c)
            x = jnp.where(beyond, after[c // 2], word)
            x, b = (upper(x), lower(word)) if c % 2 else (lower(x), upper(word))
            x, b = x.astype(F32), b.astype(F32)
            x = x * x
            b = b * b
            values.append(b + away * (x - b))
        return values

    def wait_chunk(c, n=1):
        here = rb.at[pl.ds(c, n), pl.ds(0, ND * CHUNK), :]
        pltpu.make_async_copy(here, here, brecv.at[c]).wait()

    def store_sums(g, t, s):
        for z in range(GROUP):
            plane = GROUP * g + z
            value = s[XT * z : XT * (z + 1)]
            sbuf[plane] = value + jnp.where(is_edge, edges[t, plane], pltpu.roll(value, LANES - 1, 1))

    def column_tile(o, _):
        t = jnp.where(o == 0, 2, jnp.where(o == 1, 3, 3 - o))

        @pl.when(o == 0)
        def _():
            pltpu.make_async_copy(hb, hb, hrecv).wait()
            front, back = make_edges(pair[0:XH, :], pair[XH:XB, :], hb[...], low32)
            for t in range(NC - 1):
                place_edges(t, front[XT * t : XT * (t + 1)], back[XT * t : XT * (t + 1)])
            wait_chunk(2, 2)

        @pl.when(o == 1)
        def _():
            @pl.when(has_right)
            def _():
                pltpu.make_async_copy(cb, cb, crecv).wait()

            hcb[0 : ND * TILE, :] = (hb[...].astype(F32) + cb[...].astype(F32)).astype(BF16)
            place_edges(NC - 1, *make_edges(pair[XH - XT : XH, :], pair[XB - XT : XB, :], hcb[0 : ND * TILE, :], low8))
            for g in range(NZ // GROUP):
                at = GROUP * XT * g
                tiles = hcb[2 * TILE * g : 2 * TILE * g + SIDE, :]
                store_sums(g, NC - 1, nn_dot(side_band[...], jnp.concatenate([rb[NC - 1, at : at + DEPTH, :], tiles], 0)))

        @pl.when(o == 2)
        def _():
            wait_chunk(1)

        @pl.when(o == 3)
        def _():
            wait_chunk(0)

        cols = pl.ds(pl.multiple_of(XT * t, XT), XT)
        @pl.when(o != 1)
        def _():
            for g in range(NZ // GROUP):
                at = GROUP * XT * g
                data = jnp.concatenate([rb[t, at : at + DEPTH, :], rb[t + 1, at : at + DEPTH, :]], 0)
                store_sums(g, t, nn_dot(band[...], data))

        entry_here = ent[cols, :]

        def planes(i, carry):
            cum, bright, acc = carry
            acc = list(acc)
            for p in range(PLANES):
                plane = PLANES * i + p
                colour = lookup(sbuf[plane])
                cum = cum + jnp.where(entry_here <= plane, colour[3], 0.0)
                bright_next = jnp.exp2(cum * OPTICAL)
                weight = bright - bright_next
                bright = bright_next
                for c in range(3):
                    acc[c] = acc[c] + weight * colour[c]
            return cum, bright, tuple(acc)

        _, bright, acc = lax.fori_loop(0, NZ // PLANES, planes, (zero, one, (zero,) * 3))
        for c in range(3):
            result[c, cols, :] = acc[c] * (UNIT * UNIT)
        result[3, cols, :] = bright
        return 0

    lax.fori_loop(0, NC, column_tile, 0)
    sent = pk.at[:, pl.ds(0, ND - 1)]
    pltpu.make_async_copy(sent, sent, bsend).wait()
    tiles = hk.at[pl.ds(0, ND - 1)]
    pltpu.make_async_copy(tiles, tiles, hsend).wait()

    @pl.when(has_left)
    def _():
        pltpu.make_async_copy(ck, ck, csend).wait()


def shards(volume, entry_depth, tf_table):
    dma = pltpu.SemaphoreType.DMA
    planes = pl.pallas_call(
        kernel,
        out_shape=jax.ShapeDtypeStruct((4, XH, LANES), F32),
        in_specs=[
            pl.BlockSpec(memory_space=pl.ANY),
            pl.BlockSpec(memory_space=pl.ANY),
            pl.BlockSpec(memory_space=pl.ANY),
        ],
        out_specs=pl.BlockSpec(memory_space=pltpu.VMEM),
        scratch_shapes=[
            pltpu.VMEM((ZB, XB, NY), BF16),
            pltpu.VMEM((XB, LANES), I32),
            pltpu.VMEM((4, 2 * LANES), F32),
            pltpu.VMEM((NC, ND, CHUNK, LANES), BF16),
            pltpu.VMEM((ND, TILE, LANES), BF16),
            pltpu.VMEM((ND, TILE, LANES), BF16),
            pltpu.VMEM((NC, (ND + 1) * CHUNK, LANES), BF16),
            pltpu.VMEM((ND * TILE, LANES), BF16),
            pltpu.VMEM((ND * TILE, LANES), BF16),
            pltpu.VMEM(((ND + 2) * TILE, LANES), BF16),
            pltpu.VMEM((6, 8, LANES), I32),
            pltpu.VMEM((XH, LANES), I32),
            pltpu.VMEM((GROUP * XT, 2 * DEPTH), BF16),
            pltpu.VMEM((GROUP * XT, DEPTH + SIDE), BF16),
            pltpu.VMEM((XB, LANES), BF16),
            pltpu.VMEM((NC, NZ, XT, LANES), F32),
            pltpu.VMEM((NZ, XT, LANES), F32),
            dma((4,)), dma, dma, dma, dma, dma,
            dma((NC,)), dma, dma, pltpu.SemaphoreType.REGULAR,
        ],
        compiler_params=pltpu.CompilerParams(collective_id=0, has_side_effects=True),
        name="render",
    )(volume, entry_depth, tf_table.T)
    return planes.reshape(4, XH, 2, YB).transpose(0, 3, 2, 1).reshape(4, YB, XB)


def solution(mesh):
    placed = (P("depth", "img", None), P("img", None), P())
    return jax.shard_map(
        shards, mesh=mesh, in_specs=placed, out_specs=P(None, "depth", "img"), check_vma=False
    )
```
